256 devices in a mesh: gx: 32 (over z_lo, y, core), gy: 8 (over z_hi, x).
Axes of the slice: x: 4, y: 4, z: 8 (z_hi: 2, z_lo: 4; z = z_hi * 4 + z_lo), core: 2. Of those that a mesh axis runs over, the one named last changes fastest.
Arguments:
- tokens: bfloat16 [2048, 6144], P('gx', 'gy'), may hold values from -30 to 30
- ln_gain: float32 [6144], P('gy'), may hold values from 0.1 to 1.9
- oft_skew: float32 [8, 24, 256, 256], P(None, 'gy'), may hold values from -0.375 to 0.375
- tenant_of_image: int32 [8], replicated, may hold values from 0 to 7
- w_qkv: bfloat16 [6144, 32, 3, 128], P('gy', 'gx'), may hold values from -0.076546554 to 0.076546554
- w_up: bfloat16 [6144, 24576], P('gy', 'gx'), may hold values from -0.078125 to 0.078125
- up_bias: float32 [24576], P('gx'), may hold values from -3 to 3
- q_gain: float32 [32, 128], P('gx'), may hold values from 0.8 to 5
- k_gain: float32 [32, 128], P('gx'), may hold values from 0.8 to 5
- w_out: bfloat16 [32, 128, 6144], P('gx', None, 'gy'), may hold values from -0.09375 to 0.09375
- w_down: bfloat16 [24576, 6144], P('gx', 'gy'), may hold values from -0.0390625 to 0.0390625
- down_bias: float32 [6144], P('gy'), may hold values from -3 to 3
Outputs:
- layer_out: bfloat16 [2048, 6144], P('gx', 'gy')
The draws below stay inside these ranges and needn't reach their ends.
All inputs are finite; a program needn't handle non-finite values.
Results may differ from the reference program's by a relative error of at most 0.005.
Values may be sent and summed in bfloat16 or wider, within the bound.
No kernel may reach another device: no remote copies, remote signals or barrier semaphores. Data moves between devices by JAX's collectives and lax.ppermute only.
A program may use at most 64 MiB of HBM per device.

```python
import jax
import jax.numpy as jnp
from jax import lax

D = 6144
FF = 24576
DH = 128
HEADS = 32
OFT_BLOCK = 256
TENANTS = 8
PATCHES = 256
IMAGES = 8
TOKENS = 2048


def draw_tokens(key, part):
    first, second = jax.random.split(key, 2)
    column_scale = 0.5 * 3.0 ** (jnp.arange(D, dtype=jnp.float32) / D)
    column_scale = column_scale[None, :] * jax.random.uniform(second, (1, D), jnp.float32, 0.7, 1.3)
    drawn = jax.random.normal(first, (TOKENS, D), jnp.float32) * column_scale
    return jnp.clip(drawn, -30.0, 30.0).astype(jnp.bfloat16)


def draw_oft_skew(key, part):
    first = jax.random.fold_in(jax.random.fold_in(key, 37), 0)
    block_count = D // OFT_BLOCK
    shape = (TENANTS, block_count, OFT_BLOCK, OFT_BLOCK)
    drawn = jax.random.uniform(first, shape, jnp.float32, -0.375, 0.375)
    return drawn.astype(jnp.float32)


def draw_w_qkv(key, part):
    first = jax.random.fold_in(key, 0)
    base = jnp.clip(jax.random.normal(first, (D, HEADS, 3, DH), jnp.float32), -5.5, 5.5)
    return (base * D ** (-0.5)).astype(jnp.bfloat16)


def gain_draw(key, salt):
    folded = jax.random.fold_in(key, salt)
    second = jax.random.fold_in(folded, 1)
    return jax.random.uniform(second, (HEADS, DH), jnp.float32, 0.8, 1.6)


def draw_q_gain(key, part):
    return gain_draw(key, 11)


def draw_k_gain(key, part):
    return gain_draw(key, 23)


def plant(result, key, least, largest):
    longest = result.shape.index(max(result.shape))
    spots = []
    for shift in (0, 1):
        where = [jax.random.randint(jax.random.fold_in(key, axis), (), 0, length) for axis, length in enumerate(result.shape)]
        where[longest] = (where[longest] + shift) % result.shape[longest]
        spots.append(tuple(where))
    return result.at[spots[0]].set(least).at[spots[1]].set(largest)


def block_scale(rng, dims, shards, least, top_value):
    loudness, own = 1.0, jax.random.fold_in(rng, 6)
    for dim, blocks in shards:
        draws = jnp.exp(jax.random.uniform(jax.random.fold_in(own, dim), (blocks,), jnp.float32, least / len(shards), top_value / len(shards)))
        loudness = loudness * jnp.repeat(draws, dims[dim] // blocks).reshape([-1 if axis == dim else 1 for axis in range(len(dims))])
    return loudness


def bell_draw(key, dims, scale, reach, shards=(), kind=jnp.bfloat16):
    values = scale * jax.random.normal(key, dims, jnp.float32)
    if shards:
        values = values * block_scale(key, dims, shards, -0.22, 0.18)
    return jnp.clip(values, -reach, reach).astype(kind)


def setup_inputs(seed: int = 0) -> dict:
    key_of = jax.random.split(jax.random.key(seed), 13)
    tokens = draw_tokens(jax.random.fold_in(key_of[12], 71), 0)
    ln_gain = jnp.clip(1.0 + 0.18 * jax.random.normal(key_of[1], (D,), jnp.float32), 0.1, 1.9)
    oft_skew = draw_oft_skew(jax.random.fold_in(key_of[12], 71), 0)
    tenant_of_image = plant(jax.random.randint(key_of[3], (IMAGES,), 0, TENANTS), jax.random.fold_in(key_of[3], 1), 0, TENANTS - 1).astype(jnp.int32)
    w_qkv = draw_w_qkv(jax.random.fold_in(key_of[12], 71), 0)
    w_up = bell_draw(key_of[5], (D, FF), D ** -0.5, 0.078125, ((0, 8), (1, 32)))
    up_bias = bell_draw(key_of[6], (FF,), 0.5, 3.0, ((0, 32),), jnp.float32)
    q_gain = draw_q_gain(jax.random.fold_in(key_of[12], 71), 0)
    k_gain = draw_k_gain(jax.random.fold_in(key_of[12], 71), 0)
    w_out = bell_draw(key_of[9], (HEADS, DH, D), (HEADS * DH) ** -0.5, 0.09375, ((0, 32), (2, 8)))
    w_down = bell_draw(key_of[10], (FF, D), FF ** -0.5, 0.0390625, ((0, 32), (1, 8)))
    down_bias = bell_draw(key_of[11], (D,), 0.5, 3.0, ((0, 8),), jnp.float32)
    return dict(tokens=tokens, ln_gain=ln_gain, oft_skew=oft_skew, tenant_of_image=tenant_of_image, w_qkv=w_qkv, w_up=w_up, up_bias=up_bias, q_gain=q_gain, k_gain=k_gain, w_out=w_out, w_down=w_down, down_bias=down_bias)


HIGH = lax.Precision.HIGHEST

def cayley(skew_raw):
    skew_part = 0.5 * (skew_raw - jnp.swapaxes(skew_raw, -1, -2))
    identity = jnp.eye(skew_part.shape[-1], dtype=jnp.float32)
    plus_skew = identity + skew_part
    gram_matrix = identity - jnp.matmul(skew_part, skew_part, precision=HIGH)
    factor = jnp.linalg.cholesky(gram_matrix)
    lower_solved = lax.linalg.triangular_solve(factor, plus_skew, left_side=True, lower=True)
    solved = lax.linalg.triangular_solve(factor, lower_solved, left_side=True, lower=True, transpose_a=True)
    return jnp.matmul(plus_skew, solved, precision=HIGH)

def norm_last(values_in, gain):
    width_count = values_in.shape[-1]
    row_mean = lax.optimization_barrier(jnp.sum(values_in, -1, keepdims=True)) / width_count
    row_var = lax.optimization_barrier(jnp.sum(values_in * values_in, -1, keepdims=True)) / width_count - row_mean * row_mean
    return (values_in - row_mean) * lax.rsqrt(row_var + 1e-06) * gain

def reference(tokens, ln_gain, oft_skew, tenant_of_image, w_qkv, w_up, up_bias, q_gain, k_gain, w_out, w_down, down_bias):
    floats = tokens.astype(jnp.float32)
    normed = norm_last(floats, ln_gain)
    block_count = D // OFT_BLOCK
    rotations = cayley(oft_skew.reshape(TENANTS * block_count, OFT_BLOCK, OFT_BLOCK))
    rotations = rotations.reshape(TENANTS, block_count, OFT_BLOCK, OFT_BLOCK)
    chosen = rotations[tenant_of_image.astype(jnp.int32)]
    blocks = normed.reshape(IMAGES, PATCHES, block_count, OFT_BLOCK)
    turned = jnp.einsum('ipnb,incb->ipnc', blocks, chosen, precision=HIGH)
    turned = turned.reshape(TOKENS, D).astype(jnp.bfloat16)
    projected = jnp.dot(turned.astype(jnp.float32), w_qkv.reshape(D, HEADS * 3 * DH).astype(jnp.float32), preferred_element_type=jnp.float32)
    projected = projected.reshape(IMAGES, PATCHES, HEADS, 3, DH)
    up_pre = jnp.dot(turned.astype(jnp.float32), w_up.astype(jnp.float32), preferred_element_type=jnp.float32)
    queries = norm_last(projected[:, :, :, 0, :], q_gain).astype(jnp.bfloat16)
    keys_normed = norm_last(projected[:, :, :, 1, :], k_gain).astype(jnp.bfloat16)
    values = projected[:, :, :, 2, :].astype(jnp.bfloat16)
    scores = jnp.einsum('iphd,iqhd->ihpq', queries.astype(jnp.float32), keys_normed.astype(jnp.float32)) / jnp.sqrt(jnp.float32(DH))
    top_score = lax.optimization_barrier(jnp.max(scores, -1, keepdims=True))
    expo = jnp.exp(scores - top_score)
    weights = (expo / lax.optimization_barrier(jnp.sum(expo, -1, keepdims=True))).astype(jnp.bfloat16)
    attended = jnp.einsum('ihpq,iqhd->iphd', weights.astype(jnp.float32), values.astype(jnp.float32))
    attended = attended.astype(jnp.bfloat16).reshape(TOKENS, HEADS * DH)
    hidden = jax.nn.gelu(up_pre + up_bias, approximate=False).astype(jnp.bfloat16)
    mixed = jnp.dot(attended.astype(jnp.float32), w_out.reshape(HEADS * DH, D).astype(jnp.float32), preferred_element_type=jnp.float32)
    mixed = mixed + jnp.dot(hidden.astype(jnp.float32), w_down.astype(jnp.float32), preferred_element_type=jnp.float32)
    return (floats + mixed + down_bias).astype(jnp.bfloat16)
```

```python
import functools

import jax
import jax.numpy as jnp
from jax import lax
from jax.experimental import pallas as pl
from jax.experimental.pallas import tpu as pltpu
from jax.sharding import Mesh
from jax.sharding import PartitionSpec as P

PATCHES = 256
HIGH = lax.Precision.HIGHEST
AXES = (("zl", 4), ("y", 4), ("core", 2), ("zh", 2), ("x", 4))
CHIPS = ("zl", "y")
GX = ("zl", "y", "core")
GY = ("zh", "x")


def split_bf16(value):
    high = value.astype(jnp.bfloat16)
    low = (value - high.astype(jnp.float32)).astype(jnp.bfloat16)
    return high, low

def dot3(left, right):
    left_high, left_low = left
    right_high, right_low = right
    return jnp.dot(
        jnp.concatenate([left_high, left_high, left_low], 1),
        jnp.concatenate([right_high, right_low, right_high], 0),
        preferred_element_type=jnp.float32,
    )

def cayley_kernel(tenant_ref, raw_ref, rotation_ref, skew_ref, inverse_ref):
    count, order = raw_ref.shape[1], raw_ref.shape[2]
    identity = (
        lax.broadcasted_iota(jnp.int32, (order, order), 0)
        == lax.broadcasted_iota(jnp.int32, (order, order), 1)
    ).astype(jnp.float32)
    bounds = []
    for block in range(count):
        raw = raw_ref[0, block]
        skew = 0.5 * (raw.T - raw)
        parts = split_bf16(skew)
        skew_ref[block] = skew
        gram = identity - dot3(parts, parts)
        bounds.append(1.001 * jnp.sqrt(0.5 * jnp.sum(gram * gram, keepdims=True)))
        inverse_ref[block] = gram
    top = functools.reduce(jnp.maximum, bounds)
    least = 1.0 / top
    scale = 2.0 * top / (1.0 + top)
    for block in range(count):
        start = (identity + skew_ref[block]) * least
        ratio = inverse_ref[block] * (least * scale)
        update = dot3(split_bf16(start), split_bf16(ratio))
        inverse_ref[block] = scale * (2.0 * start - update)
    least = 4.0 * top / ((1.0 + top) * (1.0 + top))

    def step(scale):
        for block in range(count):
            inverse = inverse_ref[block]
            parts = split_bf16(inverse)
            product = inverse - dot3(split_bf16(skew_ref[block]), parts)
            update = dot3(parts, split_bf16(product * scale))
            inverse_ref[block] = scale * (2.0 * inverse - update)

    def keep_going(carry):
        return carry[0, 0] < 0.97

    def scaled_step(carry):
        step(2.0 / (1.0 + carry))
        return 4.0 * carry / ((1.0 + carry) * (1.0 + carry))

    lax.while_loop(keep_going, scaled_step, least)
    step(jnp.ones((1, 1), jnp.float32))
    for block in range(count):
        inverse = inverse_ref[block]
        skew = skew_ref[block]
        rest = identity - inverse + jnp.dot(skew, inverse, precision=HIGH, preferred_element_type=jnp.float32)
        fixed = inverse + dot3(split_bf16(inverse), split_bf16(rest))
        rotation_ref[block] = 2.0 * fixed - identity

def cayley(tenant, oft_skew):
    count, order = oft_skew.shape[1], oft_skew.shape[2]
    return pl.pallas_call(
        cayley_kernel,
        out_shape=jax.ShapeDtypeStruct((count, order, order), jnp.float32),
        grid_spec=pltpu.PrefetchScalarGridSpec(
            num_scalar_prefetch=1,
            grid=(1,),
            in_specs=[pl.BlockSpec((1, count, order, order), lambda i, tenant: (tenant[0], 0, 0, 0))],
            out_specs=pl.BlockSpec((count, order, order), lambda i, tenant: (0, 0, 0)),
            scratch_shapes=[
                pltpu.VMEM((count, order, order), jnp.float32),
                pltpu.VMEM((count, order, order), jnp.float32),
            ],
        ),
        compiler_params=pltpu.CompilerParams(vmem_limit_bytes=24 << 20),
        cost_estimate=pl.CostEstimate(flops=20_000_000_000, bytes_accessed=2_000_000, transcendentals=0),
    )(tenant, oft_skew)


def rotate_kernel(tokens_ref, mean_ref, scale_ref, gain_ref, rotation_ref, turned_ref):
    order = rotation_ref.shape[1]
    for block in range(rotation_ref.shape[0]):
        columns = pl.ds(block * order, order)
        floats = tokens_ref[:, columns].astype(jnp.float32)
        normed = (floats - mean_ref[...]) * scale_ref[...] * gain_ref[:, columns]
        turned_ref[:, columns] = jnp.dot(
            normed, rotation_ref[block], precision=HIGH, preferred_element_type=jnp.float32
        ).astype(jnp.bfloat16)


def rotate(tokens, row_mean, row_scale, gain, rotation):
    return pl.pallas_call(
        rotate_kernel,
        out_shape=jax.ShapeDtypeStruct(tokens.shape, jnp.bfloat16),
        cost_estimate=pl.CostEstimate(
            flops=600_000_000, bytes_accessed=1_000_000, transcendentals=0
        ),
    )(tokens, row_mean, row_scale, gain, rotation)


def head_norm(values_in, gain):
    width_count = values_in.shape[-1]
    row_mean = jnp.sum(values_in, -1, keepdims=True) / width_count
    row_var = jnp.sum(values_in * values_in, -1, keepdims=True) / width_count - row_mean * row_mean
    return (values_in - row_mean) * lax.rsqrt(row_var + 1e-06) * gain


def swap(value):
    return lax.ppermute(value, "core", [(0, 1), (1, 0)])


def spread(value, axes):
    copies = jnp.broadcast_to(value[None], (lax.axis_size(axes), *value.shape))
    return lax.all_to_all(copies, axes, 0, 0, tiled=True)


def reduce_blocks(partial, axes):
    group = lax.axis_size(axes)
    blocks = partial.astype(jnp.bfloat16).reshape(group, partial.shape[0] // group, partial.shape[1])
    return jnp.sum(lax.all_to_all(blocks, axes, 0, 0, tiled=True).astype(jnp.float32), 0)


def matmul(left, right):
    return jnp.dot(left, right, preferred_element_type=jnp.float32)


def per_device(
    tokens,
    ln_gain,
    oft_skew,
    tenant_of_image,
    w_qkv,
    w_up,
    up_bias,
    q_gain,
    k_gain,
    w_out,
    w_down,
    down_bias,
):
    row_count, local_width = tokens.shape
    head_dim = w_qkv.shape[3]
    qkv_cols = 3 * head_dim

    qkv_own = w_qkv.reshape(local_width, qkv_cols)
    out_own = w_out.reshape(head_dim, w_out.shape[2])
    small_own = jnp.concatenate([up_bias[None], q_gain, k_gain], 1)
    small = jnp.concatenate([small_own, swap(small_own)], 0)
    qkv_both = jnp.concatenate([qkv_own, swap(qkv_own)], 1)
    up_both = jnp.concatenate([w_up, swap(w_up)], 1)
    down_both = jnp.concatenate([w_down, swap(w_down)], 0)
    out_both = jnp.concatenate([out_own, swap(out_own)], 0)
    hidden_width = up_bias.shape[0]
    bias_both = small[:, :hidden_width].reshape(1, 2 * hidden_width)
    q_gain_both = small[:, hidden_width : hidden_width + head_dim]
    k_gain_both = small[:, hidden_width + head_dim :]

    full_width = local_width * lax.axis_size(GY)
    floats = tokens.astype(jnp.float32)
    row_sums = jnp.stack([jnp.sum(floats, 1), jnp.sum(floats * floats, 1)])
    row_sums = jnp.sum(spread(row_sums, GY), 0)
    row_mean = row_sums[0][:, None] / full_width
    row_var = row_sums[1][:, None] / full_width - row_mean * row_mean
    row_scale = lax.rsqrt(row_var + 1e-06)

    patches = PATCHES
    image_index = lax.axis_index(GX) * row_count // patches
    tenant = lax.dynamic_slice_in_dim(tenant_of_image, image_index, 1, 0)
    rotation = cayley(tenant, oft_skew)
    turned = rotate(tokens, row_mean, row_scale, ln_gain[None], rotation)

    gathered = spread(turned, CHIPS).reshape(-1, local_width)
    qkv = reduce_blocks(matmul(gathered, qkv_both), GY)
    up_pre = reduce_blocks(matmul(gathered, up_both), GY)

    half = qkv.shape[0]
    parts = qkv.reshape(half, 2, 3, head_dim)
    queries = head_norm(parts[:, :, 0], q_gain_both).astype(jnp.bfloat16)
    keys_normed = head_norm(parts[:, :, 1], k_gain_both).astype(jnp.bfloat16)
    values = parts[:, :, 2].astype(jnp.bfloat16)
    pair = jnp.stack([keys_normed, values], 2)
    pair = jnp.concatenate([pair, swap(pair)[:, ::-1]], 0)
    scores = jnp.einsum(
        "phd,qhd->hpq", queries, pair[:, :, 0], preferred_element_type=jnp.float32
    ) / jnp.sqrt(jnp.float32(head_dim))
    top_score = jnp.max(scores, -1, keepdims=True)
    expo = jnp.exp(scores - top_score)
    weights = (expo / jnp.sum(expo, -1, keepdims=True)).astype(jnp.bfloat16)
    attended = jnp.einsum("hpq,qhd->phd", weights, pair[:, :, 1], preferred_element_type=jnp.float32)
    attended = attended.astype(jnp.bfloat16).reshape(half, 2 * head_dim)
    hidden = jax.nn.gelu(up_pre + bias_both, approximate=False).astype(jnp.bfloat16)

    all_hidden = spread(hidden, GY).reshape(-1, hidden.shape[1])
    all_attended = spread(attended, GY).reshape(-1, attended.shape[1])
    mixed = reduce_blocks(matmul(all_hidden, down_both) + matmul(all_attended, out_both), CHIPS)
    return (floats + mixed + down_bias).astype(jnp.bfloat16)


def solution(mesh):
    names = tuple(name for name, _ in AXES)
    sizes = tuple(size for _, size in AXES)
    fine_mesh = Mesh(mesh.devices.reshape(sizes), names)
    in_specs = (
        P(GX, GY),
        P(GY),
        P(None, GY, None, None),
        P(),
        P(GY, GX, None, None),
        P(GY, GX),
        P(GX),
        P(GX, None),
        P(GX, None),
        P(GX, None, GY),
        P(GX, GY),
        P(GY),
    )
    return jax.shard_map(
        per_device, mesh=fine_mesh, in_specs=in_specs, out_specs=P(GX, GY), check_vma=False
    )
```

```python
import functools

import jax
import jax.numpy as jnp
from jax import lax
from jax.experimental import pallas as pl
from jax.experimental.pallas import tpu as pltpu
from jax.sharding import Mesh
from jax.sharding import PartitionSpec as P

PATCHES = 256
HIGH = lax.Precision.HIGHEST
AXES = (("zl", 4), ("y", 4), ("core", 2), ("zh", 2), ("x", 4))
CHIPS = ("zl", "y")
GX = ("zl", "y", "core")
GY = ("zh", "x")


def split_bf16(value):
    high = value.astype(jnp.bfloat16)
    low = (value - high.astype(jnp.float32)).astype(jnp.bfloat16)
    return high, low

def dot3(left, right):
    left_high, left_low = left
    right_high, right_low = right
    return jnp.dot(
        jnp.concatenate([left_high, left_high, left_low], 1),
        jnp.concatenate([right_high, right_low, right_high], 0),
        preferred_element_type=jnp.float32,
    )

def cayley_kernel(tenant_ref, raw_ref, rotation_ref, skew_ref, inverse_ref):
    count, order = raw_ref.shape[1], raw_ref.shape[2]
    identity = (
        lax.broadcasted_iota(jnp.int32, (order, order), 0)
        == lax.broadcasted_iota(jnp.int32, (order, order), 1)
    ).astype(jnp.float32)
    bounds = []
    for block in range(count):
        raw = raw_ref[0, block]
        skew = 0.5 * (raw.T - raw)
        parts = split_bf16(skew)
        skew_ref[block] = skew
        gram = identity - dot3(parts, parts)
        bounds.append(1.001 * jnp.sqrt(0.5 * jnp.sum(gram * gram, keepdims=True)))
        inverse_ref[block] = gram
    top = functools.reduce(jnp.maximum, bounds)
    least = 1.0 / top
    scale = 2.0 * top / (1.0 + top)
    for block in range(count):
        start = (identity + skew_ref[block]) * least
        ratio = inverse_ref[block] * (least * scale)
        update = dot3(split_bf16(start), split_bf16(ratio))
        inverse_ref[block] = scale * (2.0 * start - update)
    least = 4.0 * top / ((1.0 + top) * (1.0 + top))

    def step(scale):
        for block in range(count):
            inverse = inverse_ref[block]
            parts = split_bf16(inverse)
            product = inverse - dot3(split_bf16(skew_ref[block]), parts)
            update = dot3(parts, split_bf16(product * scale))
            inverse_ref[block] = scale * (2.0 * inverse - update)

    def keep_going(carry):
        return carry[0, 0] < 0.97

    def scaled_step(carry):
        step(2.0 / (1.0 + carry))
        return 4.0 * carry / ((1.0 + carry) * (1.0 + carry))

    lax.while_loop(keep_going, scaled_step, least)
    step(jnp.ones((1, 1), jnp.float32))
    for block in range(count):
        inverse = inverse_ref[block]
        skew = skew_ref[block]
        rest = identity - inverse + jnp.dot(skew, inverse, precision=HIGH, preferred_element_type=jnp.float32)
        fixed = inverse + dot3(split_bf16(inverse), split_bf16(rest))
        rotation_ref[block] = 2.0 * fixed - identity

def cayley(tenant, oft_skew):
    count, order = oft_skew.shape[1], oft_skew.shape[2]
    return pl.pallas_call(
        cayley_kernel,
        out_shape=jax.ShapeDtypeStruct((count, order, order), jnp.float32),
        grid_spec=pltpu.PrefetchScalarGridSpec(
            num_scalar_prefetch=1,
            grid=(1,),
            in_specs=[pl.BlockSpec((1, count, order, order), lambda i, tenant: (tenant[0], 0, 0, 0))],
            out_specs=pl.BlockSpec((count, order, order), lambda i, tenant: (0, 0, 0)),
            scratch_shapes=[
                pltpu.VMEM((count, order, order), jnp.float32),
                pltpu.VMEM((count, order, order), jnp.float32),
            ],
        ),
        compiler_params=pltpu.CompilerParams(vmem_limit_bytes=60 << 20),
        cost_estimate=pl.CostEstimate(flops=20_000_000_000, bytes_accessed=2_000_000, transcendentals=0),
    )(tenant, oft_skew)


def rotate_kernel(full_width, tokens_ref, sums_ref, gain_ref, rotation_ref, turned_ref):
    copies, rows = turned_ref.shape[0], tokens_ref.shape[0]
    order = rotation_ref.shape[1]
    sums = jnp.broadcast_to(jnp.sum(sums_ref[...], 0), (rows, 2 * rows))
    lane = lax.broadcasted_iota(jnp.int32, sums.shape, 1)
    row = lax.broadcasted_iota(jnp.int32, sums.shape, 0)
    total = jnp.sum(jnp.where(lane == row, sums, 0.0), 1, keepdims=True)
    squares = jnp.sum(jnp.where(lane == row + rows, sums, 0.0), 1, keepdims=True)
    row_mean = total / full_width
    row_var = squares / full_width - row_mean * row_mean
    row_scale = lax.rsqrt(row_var + 1e-06)
    for block in range(rotation_ref.shape[0]):
        columns = pl.ds(block * order, order)
        floats = tokens_ref[:, columns].astype(jnp.float32)
        normed = (floats - row_mean) * row_scale * gain_ref[:, columns]
        turned = jnp.dot(
            normed, rotation_ref[block], precision=HIGH, preferred_element_type=jnp.float32
        ).astype(jnp.bfloat16)
        for copy in range(copies):
            turned_ref[copy, :, columns] = turned


def rotate(tokens, sums, gain, rotation, full_width, copies):
    return pl.pallas_call(
        functools.partial(rotate_kernel, full_width),
        out_shape=jax.ShapeDtypeStruct((copies, *tokens.shape), jnp.bfloat16),
        cost_estimate=pl.CostEstimate(
            flops=600_000_000, bytes_accessed=3_000_000, transcendentals=0
        ),
    )(tokens, sums, gain, rotation)


def head_norm(values_in, gain):
    width_count = values_in.shape[-1]
    row_mean = jnp.sum(values_in, -1, keepdims=True) / width_count
    row_var = jnp.sum(values_in * values_in, -1, keepdims=True) / width_count - row_mean * row_mean
    return (values_in - row_mean) * lax.rsqrt(row_var + 1e-06) * gain


def heads_kernel(parts_ref, q_gain_ref, k_gain_ref, queries_ref, pair_ref):
    head_dim = q_gain_ref.shape[-1]
    qkv = parts_ref[0].astype(jnp.float32)
    for part in range(1, parts_ref.shape[0]):
        qkv = qkv + parts_ref[part].astype(jnp.float32)
    queries = head_norm(qkv[:, :head_dim], q_gain_ref[0])
    keys_normed = head_norm(qkv[:, head_dim : 2 * head_dim], k_gain_ref[0])
    queries_ref[0] = queries.astype(jnp.bfloat16)
    pair_ref[0, 0] = keys_normed.astype(jnp.bfloat16)
    pair_ref[0, 1] = qkv[:, 2 * head_dim :].astype(jnp.bfloat16)


def heads(received, q_gain, k_gain, step):
    group, rows, _ = received.shape
    head_dim = q_gain.shape[-1]
    return pl.pallas_call(
        heads_kernel,
        out_shape=(
            jax.ShapeDtypeStruct((2, rows, head_dim), jnp.bfloat16),
            jax.ShapeDtypeStruct((2, 2, rows, head_dim), jnp.bfloat16),
        ),
        grid=(2,),
        in_specs=[
            pl.BlockSpec((group, rows, 3 * head_dim), lambda head: (0, 0, step * head)),
            pl.BlockSpec((1, 1, head_dim), lambda head: (head, 0, 0)),
            pl.BlockSpec((1, 1, head_dim), lambda head: (head, 0, 0)),
        ],
        out_specs=(
            pl.BlockSpec((1, rows, head_dim), lambda head: (head, 0, 0)),
            pl.BlockSpec((1, 2, rows, head_dim), lambda head: (head, 0, 0, 0)),
        ),
        cost_estimate=pl.CostEstimate(
            flops=10_000_000, bytes_accessed=2_000_000, transcendentals=0
        ),
    )(received, q_gain, k_gain)


def attention_kernel(queries_ref, pair_ref, other_ref, near_ref, far_ref, mixed_in_ref):
    copies = mixed_in_ref.shape[0]
    head_dim = queries_ref.shape[-1]
    width = near_ref.shape[-1]
    for head in range(2):
        keys = jnp.concatenate([pair_ref[head, 0], other_ref[1 - head, 0]], 0)
        values = jnp.concatenate([pair_ref[head, 1], other_ref[1 - head, 1]], 0)
        scores = lax.dot_general(
            queries_ref[head], keys, (((1,), (1,)), ((), ())), preferred_element_type=jnp.float32
        ) / jnp.sqrt(jnp.float32(head_dim))
        expo = jnp.exp(scores - jnp.max(scores, -1, keepdims=True))
        weights = (expo / jnp.sum(expo, -1, keepdims=True)).astype(jnp.bfloat16)
        attended = jnp.dot(weights, values, preferred_element_type=jnp.float32).astype(jnp.bfloat16)
        start = head * (width + head_dim)
        for copy in range(copies):
            mixed_in_ref[copy, :, start : start + width] = (near_ref, far_ref)[head][...]
            mixed_in_ref[copy, :, start + width : start + width + head_dim] = attended


def attention(queries, pair, other, hidden, copies):
    rows, width = hidden[0].shape
    return pl.pallas_call(
        attention_kernel,
        out_shape=jax.ShapeDtypeStruct((copies, rows, 2 * (width + queries.shape[-1])), jnp.bfloat16),
        compiler_params=pltpu.CompilerParams(vmem_limit_bytes=60 << 20),
        cost_estimate=pl.CostEstimate(
            flops=40_000_000, bytes_accessed=5_000_000, transcendentals=70_000
        ),
    )(queries, pair, other, *hidden)


def swap(value):
    return lax.ppermute(value, "core", [(0, 1), (1, 0)])


def exchange(blocks, axes):
    return lax.all_to_all(blocks, axes, 0, 0, tiled=True)


def matmul(left, right):
    return jnp.dot(left, right, preferred_element_type=jnp.float32)


def per_device(
    tokens,
    ln_gain,
    oft_skew,
    tenant_of_image,
    w_qkv,
    w_up,
    up_bias,
    q_gain,
    k_gain,
    w_out,
    w_down,
    down_bias,
):
    row_count, local_width = tokens.shape
    head_dim = w_qkv.shape[3]
    qkv_cols = 3 * head_dim
    group = lax.axis_size(GY)
    chips = lax.axis_size(CHIPS)

    small_own = jnp.concatenate([up_bias[None], q_gain, k_gain], 1)
    first_own = jnp.concatenate([w_qkv.reshape(local_width, qkv_cols), w_up], 1)
    second_own = jnp.concatenate([w_down, w_out.reshape(head_dim, w_out.shape[2])], 0)
    small = jnp.stack([small_own, swap(small_own)])
    first = jnp.concatenate([first_own, swap(first_own)], 1)
    second = jnp.concatenate([second_own, swap(second_own)], 0)
    hidden_width = up_bias.shape[0]
    bias = small[:, 0, :hidden_width]
    q_gains = small[:, :, hidden_width : hidden_width + head_dim]
    k_gains = small[:, :, hidden_width + head_dim :]

    floats = tokens.astype(jnp.float32)
    row_sums = jnp.concatenate([jnp.sum(floats, 1), jnp.sum(floats * floats, 1)])[None, None]
    row_sums = exchange(jnp.broadcast_to(row_sums, (group, 1, 2 * row_count)), GY)

    image_index = lax.axis_index(GX) * row_count // PATCHES
    tenant = lax.dynamic_slice_in_dim(tenant_of_image, image_index, 1, 0)
    rotation = cayley(tenant, oft_skew)
    turned = rotate(tokens, row_sums, ln_gain[None], rotation, local_width * group, chips)

    gathered = exchange(turned, CHIPS).reshape(chips * row_count, local_width)
    partial_in = matmul(gathered, first).astype(jnp.bfloat16)
    half = chips * row_count // group
    received = exchange(partial_in.reshape(group, half, partial_in.shape[1]), GY)

    step = (qkv_cols + hidden_width) // qkv_cols
    queries, pair = heads(received, q_gains, k_gains, step)
    other = swap(pair)
    hidden = []
    for core in range(2):
        start = core * (qkv_cols + hidden_width) + qkv_cols
        up_pre = jnp.sum(received[:, :, start : start + hidden_width].astype(jnp.float32), 0)
        unit = jax.nn.gelu(up_pre + bias[core], approximate=False)
        hidden.append(unit.astype(jnp.bfloat16))
    mixed_in = attention(queries, pair, other, hidden, group)

    gathered_in = exchange(mixed_in, GY).reshape(group * half, mixed_in.shape[2])
    partial_out = matmul(gathered_in, second).astype(jnp.bfloat16)
    returned = exchange(partial_out.reshape(chips, row_count, partial_out.shape[1]), CHIPS)
    mixed = jnp.sum(returned.astype(jnp.float32), 0)
    return (floats + mixed + down_bias).astype(jnp.bfloat16)


def solution(mesh):
    names = tuple(name for name, _ in AXES)
    sizes = tuple(size for _, size in AXES)
    fine_mesh = Mesh(mesh.devices.reshape(sizes), names)
    in_specs = (
        P(GX, GY),
        P(GY),
        P(None, GY, None, None),
        P(),
        P(GY, GX, None, None),
        P(GY, GX),
        P(GX),
        P(GX, None),
        P(GX, None),
        P(GX, None, GY),
        P(GX, GY),
        P(GY),
    )
    return jax.shard_map(
        per_device, mesh=fine_mesh, in_specs=in_specs, out_specs=P(GX, GY), check_vma=False
    )
```

```python
import functools

import jax
import jax.numpy as jnp
from jax import lax
from jax.experimental import pallas as pl
from jax.experimental.pallas import tpu as pltpu
from jax.sharding import Mesh
from jax.sharding import PartitionSpec as P

PATCHES = 256
HIGH = lax.Precision.HIGHEST
AXES = (("zl", 4), ("y", 4), ("core", 2), ("zh", 2), ("x", 4))
CHIPS = ("zl", "y")
GX = ("zl", "y", "core")
GY = ("zh", "x")
FAR_FIRST = (2, 1, 3)


def split_bf16(value):
    high = value.astype(jnp.bfloat16)
    low = (value - high.astype(jnp.float32)).astype(jnp.bfloat16)
    return high, low

def dot3(left, right):
    left_high, left_low = left
    right_high, right_low = right
    return jnp.dot(
        jnp.concatenate([left_high, left_high, left_low], 1),
        jnp.concatenate([right_high, right_low, right_high], 0),
        preferred_element_type=jnp.float32,
    )

def cayley_kernel(tenant_ref, raw_ref, rotation_ref, skew_ref, inverse_ref):
    count, order = raw_ref.shape[1], raw_ref.shape[2]
    identity = (
        lax.broadcasted_iota(jnp.int32, (order, order), 0)
        == lax.broadcasted_iota(jnp.int32, (order, order), 1)
    ).astype(jnp.float32)
    bounds = []
    for block in range(count):
        raw = raw_ref[0, block]
        skew = 0.5 * (raw.T - raw)
        parts = split_bf16(skew)
        skew_ref[block] = skew
        gram = identity - dot3(parts, parts)
        bounds.append(1.001 * jnp.sqrt(0.5 * jnp.sum(gram * gram, keepdims=True)))
        inverse_ref[block] = gram
    top = functools.reduce(jnp.maximum, bounds)
    least = 1.0 / top
    scale = 2.0 * top / (1.0 + top)
    for block in range(count):
        start = (identity + skew_ref[block]) * least
        ratio = inverse_ref[block] * (least * scale)
        update = dot3(split_bf16(start), split_bf16(ratio))
        inverse_ref[block] = scale * (2.0 * start - update)
    least = 4.0 * top / ((1.0 + top) * (1.0 + top))

    def step(scale):
        for block in range(count):
            inverse = inverse_ref[block]
            parts = split_bf16(inverse)
            product = inverse - dot3(split_bf16(skew_ref[block]), parts)
            update = dot3(parts, split_bf16(product * scale))
            inverse_ref[block] = scale * (2.0 * inverse - update)

    def keep_going(carry):
        return carry[0, 0] < 0.97

    def scaled_step(carry):
        step(2.0 / (1.0 + carry))
        return 4.0 * carry / ((1.0 + carry) * (1.0 + carry))

    lax.while_loop(keep_going, scaled_step, least)
    step(jnp.ones((1, 1), jnp.float32))
    for block in range(count):
        inverse = inverse_ref[block]
        skew = skew_ref[block]
        rest = identity - inverse + jnp.dot(skew, inverse, precision=HIGH, preferred_element_type=jnp.float32)
        fixed = inverse + dot3(split_bf16(inverse), split_bf16(rest))
        rotation_ref[block] = 2.0 * fixed - identity

def cayley(tenant, oft_skew):
    count, order = oft_skew.shape[1], oft_skew.shape[2]
    return pl.pallas_call(
        cayley_kernel,
        out_shape=jax.ShapeDtypeStruct((count, order, order), jnp.float32),
        grid_spec=pltpu.PrefetchScalarGridSpec(
            num_scalar_prefetch=1,
            grid=(1,),
            in_specs=[pl.BlockSpec((1, count, order, order), lambda i, tenant: (tenant[0], 0, 0, 0))],
            out_specs=pl.BlockSpec((count, order, order), lambda i, tenant: (0, 0, 0)),
            scratch_shapes=[
                pltpu.VMEM((count, order, order), jnp.float32),
                pltpu.VMEM((count, order, order), jnp.float32),
            ],
        ),
        compiler_params=pltpu.CompilerParams(vmem_limit_bytes=60 << 20),
        cost_estimate=pl.CostEstimate(flops=20_000_000_000, bytes_accessed=2_000_000, transcendentals=0),
    )(tenant, oft_skew)


def rotate_kernel(full_width, tokens_ref, sums_ref, gain_ref, rotation_ref, turned_ref):
    copies, rows = turned_ref.shape[0], tokens_ref.shape[0]
    order = rotation_ref.shape[1]
    sums = jnp.broadcast_to(jnp.sum(sums_ref[...], 0), (rows, 2 * rows))
    lane = lax.broadcasted_iota(jnp.int32, sums.shape, 1)
    row = lax.broadcasted_iota(jnp.int32, sums.shape, 0)
    total = jnp.sum(jnp.where(lane == row, sums, 0.0), 1, keepdims=True)
    squares = jnp.sum(jnp.where(lane == row + rows, sums, 0.0), 1, keepdims=True)
    row_mean = total / full_width
    row_var = squares / full_width - row_mean * row_mean
    row_scale = lax.rsqrt(row_var + 1e-06)
    for block in range(rotation_ref.shape[0]):
        columns = pl.ds(block * order, order)
        floats = tokens_ref[:, columns].astype(jnp.float32)
        normed = (floats - row_mean) * row_scale * gain_ref[:, columns]
        turned = jnp.dot(
            normed, rotation_ref[block], precision=HIGH, preferred_element_type=jnp.float32
        ).astype(jnp.bfloat16)
        for copy in range(copies):
            turned_ref[copy, :, columns] = turned


def rotate(tokens, sums, gain, rotation, full_width, copies):
    return pl.pallas_call(
        functools.partial(rotate_kernel, full_width),
        out_shape=jax.ShapeDtypeStruct((copies, *tokens.shape), jnp.bfloat16),
        cost_estimate=pl.CostEstimate(
            flops=600_000_000, bytes_accessed=3_000_000, transcendentals=0
        ),
    )(tokens, sums, gain, rotation)


def head_norm(values_in, gain):
    width_count = values_in.shape[-1]
    row_mean = jnp.sum(values_in, -1, keepdims=True) / width_count
    row_var = jnp.sum(values_in * values_in, -1, keepdims=True) / width_count - row_mean * row_mean
    return (values_in - row_mean) * lax.rsqrt(row_var + 1e-06) * gain


def heads_kernel(near_ref, far_ref, q_gain_ref, k_gain_ref, queries_ref, pair_ref):
    head_dim = q_gain_ref.shape[-1]
    for head in range(2):
        columns = pl.ds(head * 3 * head_dim, 3 * head_dim)
        qkv = near_ref[:, columns] + far_ref[:, columns].astype(jnp.float32)
        queries = head_norm(qkv[:, :head_dim], q_gain_ref[head])
        keys_normed = head_norm(qkv[:, head_dim : 2 * head_dim], k_gain_ref[head])
        queries_ref[head] = queries.astype(jnp.bfloat16)
        pair_ref[head, 0] = keys_normed.astype(jnp.bfloat16)
        pair_ref[head, 1] = qkv[:, 2 * head_dim :].astype(jnp.bfloat16)


def heads(near, far, q_gain, k_gain):
    rows = near.shape[0]
    head_dim = q_gain.shape[-1]
    return pl.pallas_call(
        heads_kernel,
        out_shape=(
            jax.ShapeDtypeStruct((2, rows, head_dim), jnp.bfloat16),
            jax.ShapeDtypeStruct((2, 2, rows, head_dim), jnp.bfloat16),
        ),
        cost_estimate=pl.CostEstimate(
            flops=10_000_000, bytes_accessed=2_000_000, transcendentals=0
        ),
    )(near, far, q_gain, k_gain)


def attention_kernel(queries_ref, pair_ref, other_ref, attended_ref):
    head_dim = queries_ref.shape[-1]
    for head in range(2):
        keys = jnp.concatenate([pair_ref[head, 0], other_ref[1 - head, 0]], 0)
        values = jnp.concatenate([pair_ref[head, 1], other_ref[1 - head, 1]], 0)
        scores = lax.dot_general(
            queries_ref[head], keys, (((1,), (1,)), ((), ())), preferred_element_type=jnp.float32
        ) / jnp.sqrt(jnp.float32(head_dim))
        expo = jnp.exp(scores - jnp.max(scores, -1, keepdims=True))
        weights = (expo / jnp.sum(expo, -1, keepdims=True)).astype(jnp.bfloat16)
        attended = jnp.dot(weights, values, preferred_element_type=jnp.float32)
        attended_ref[:, head * head_dim : (head + 1) * head_dim] = attended.astype(jnp.bfloat16)


def attention(queries, pair, other):
    heads_here, rows, head_dim = queries.shape
    return pl.pallas_call(
        attention_kernel,
        out_shape=jax.ShapeDtypeStruct((rows, heads_here * head_dim), jnp.bfloat16),
        cost_estimate=pl.CostEstimate(
            flops=40_000_000, bytes_accessed=1_000_000, transcendentals=70_000
        ),
    )(queries, pair, other)


def swap(value):
    return lax.ppermute(value, "core", [(0, 1), (1, 0)])


def exchange(blocks, axes):
    return lax.all_to_all(blocks, axes, 0, 0, tiled=True)


def shift(value, axis, distance):
    size = lax.axis_size(axis)
    return lax.ppermute(value, axis, [(i, (i + distance) % size) for i in range(size)])


def sum_features(blocks, weights):
    size = len(blocks)
    partial = [matmul(blocks[k], weights).astype(jnp.bfloat16) for k in FAR_FIRST]
    sent = {k: shift(value, "x", k) for k, value in zip(FAR_FIRST, partial)}
    total = matmul(blocks[0], weights)
    for k in reversed(FAR_FIRST):
        total = total + sent[size - k].astype(jnp.float32)
    half = total.shape[0] // 2
    return total[:half], shift(total[half:].astype(jnp.bfloat16), "zh", 1), partial


def share_rows(value):
    both = jnp.concatenate([value, shift(value, "zh", 1)], 0)
    size = lax.axis_size("x")
    sent = {k: shift(both, "x", k) for k in FAR_FIRST}
    return [both] + [sent[size - k] for k in range(1, size)]


def matmul(left, right):
    return jnp.dot(left, right, preferred_element_type=jnp.float32)


def per_device(
    tokens,
    ln_gain,
    oft_skew,
    tenant_of_image,
    w_qkv,
    w_up,
    up_bias,
    q_gain,
    k_gain,
    w_out,
    w_down,
    down_bias,
):
    row_count, local_width = tokens.shape
    head_dim = w_qkv.shape[3]
    qkv_cols = 3 * head_dim
    group = lax.axis_size(GY)
    chips = lax.axis_size(CHIPS)

    small_own = jnp.concatenate([up_bias[None], q_gain, k_gain], 1)
    small = jnp.stack([small_own, swap(small_own)])
    qkv_own = w_qkv.reshape(local_width, qkv_cols)
    out_own = w_out.reshape(head_dim, w_out.shape[2])
    qkv_both = jnp.concatenate([qkv_own, swap(qkv_own)], 1)
    up_both = jnp.concatenate([w_up, swap(w_up)], 1)
    second = jnp.concatenate([w_down, swap(w_down), out_own, swap(out_own)], 0)
    hidden_width = up_bias.shape[0]
    bias = small[:, 0, :hidden_width].reshape(2 * hidden_width)
    q_gains = small[:, :, hidden_width : hidden_width + head_dim]
    k_gains = small[:, :, hidden_width + head_dim :]

    floats = tokens.astype(jnp.float32)
    row_sums = jnp.concatenate([jnp.sum(floats, 1), jnp.sum(floats * floats, 1)])[None, None]
    row_sums = exchange(jnp.broadcast_to(row_sums, (group, 1, 2 * row_count)), GY)

    image_index = lax.axis_index(GX) * row_count // PATCHES
    tenant = lax.dynamic_slice_in_dim(tenant_of_image, image_index, 1, 0)
    rotation = cayley(tenant, oft_skew)
    turned = rotate(tokens, row_sums, ln_gain[None], rotation, local_width * group, chips)

    half = chips * row_count // group
    gathered = exchange(turned, CHIPS).reshape(group, half, local_width)
    along, across = lax.axis_size("x"), lax.axis_size("zh")
    here, side = lax.axis_index("x"), lax.axis_index("zh")

    def image_at(z_step, x_step):
        return lax.rem(side + z_step, across) * along + lax.rem(here + x_step, along)

    blocks = [
        jnp.concatenate([gathered[image_at(z_step, k)] for z_step in range(across)], 0)
        for k in range(along)
    ]
    near, far, partial = sum_features(blocks, qkv_both)
    blocks = lax.optimization_barrier((blocks, partial))[0]
    queries, pair = heads(near, far, q_gains, k_gains)
    attended = attention(queries, pair, swap(pair))
    near, far, _ = sum_features(blocks, up_both)
    up_pre = near + far.astype(jnp.float32)
    hidden = jax.nn.gelu(up_pre + bias, approximate=False).astype(jnp.bfloat16)

    rows_in = share_rows(jnp.concatenate([hidden, attended], 1))
    parts = [matmul(rows, second).astype(jnp.bfloat16) for rows in rows_in]
    parts = jnp.stack(parts).reshape(along, across, half, local_width)
    parts = jnp.stack(
        [
            parts[lax.rem(along + x - here, along), lax.rem(across + z - side, across)]
            for z in range(across)
            for x in range(along)
        ]
    )
    returned = exchange(parts.reshape(chips, row_count, local_width), CHIPS)
    mixed = jnp.sum(returned.astype(jnp.float32), 0)
    return (floats + mixed + down_bias).astype(jnp.bfloat16)


def solution(mesh):
    names = tuple(name for name, _ in AXES)
    sizes = tuple(size for _, size in AXES)
    fine_mesh = Mesh(mesh.devices.reshape(sizes), names)
    in_specs = (
        P(GX, GY),
        P(GY),
        P(None, GY, None, None),
        P(),
        P(GY, GX, None, None),
        P(GY, GX),
        P(GX),
        P(GX, None),
        P(GX, None),
        P(GX, None, GY),
        P(GX, GY),
        P(GY),
    )
    return jax.shard_map(
        per_device, mesh=fine_mesh, in_specs=in_specs, out_specs=P(GX, GY), check_vma=False
    )
```

```python
import functools

import jax
import jax.numpy as jnp
from jax import lax
from jax.experimental import pallas as pl
from jax.experimental.pallas import tpu as pltpu
from jax.sharding import Mesh
from jax.sharding import PartitionSpec as P

PATCHES = 256
HIGH = lax.Precision.HIGHEST
AXES = (("zl", 4), ("y", 4), ("core", 2), ("zh", 2), ("x", 4))
GX = ("zl", "y", "core")
GY = ("zh", "x")
FAR_FIRST = (2, 1, 3)


def split_bf16(value):
    high = value.astype(jnp.bfloat16)
    low = (value - high.astype(jnp.float32)).astype(jnp.bfloat16)
    return high, low

def dot3(left, right):
    left_high, left_low = left
    right_high, right_low = right
    return jnp.dot(
        jnp.concatenate([left_high, left_high, left_low], 1),
        jnp.concatenate([right_high, right_low, right_high], 0),
        preferred_element_type=jnp.float32,
    )

def cayley_kernel(tenant_ref, raw_ref, rotation_ref, skew_ref, inverse_ref):
    count, order = raw_ref.shape[1], raw_ref.shape[2]
    identity = (
        lax.broadcasted_iota(jnp.int32, (order, order), 0)
        == lax.broadcasted_iota(jnp.int32, (order, order), 1)
    ).astype(jnp.float32)
    bounds = []
    for block in range(count):
        raw = raw_ref[0, block]
        skew = 0.5 * (raw.T - raw)
        parts = split_bf16(skew)
        skew_ref[block] = skew
        gram = identity - dot3(parts, parts)
        bounds.append(1.001 * jnp.sqrt(0.5 * jnp.sum(gram * gram, keepdims=True)))
        inverse_ref[block] = gram
    top = functools.reduce(jnp.maximum, bounds)
    least = 1.0 / top
    scale = 2.0 * top / (1.0 + top)
    for block in range(count):
        start = (identity + skew_ref[block]) * least
        ratio = inverse_ref[block] * (least * scale)
        update = dot3(split_bf16(start), split_bf16(ratio))
        inverse_ref[block] = scale * (2.0 * start - update)
    least = 4.0 * top / ((1.0 + top) * (1.0 + top))

    def step(scale):
        for block in range(count):
            inverse = inverse_ref[block]
            parts = split_bf16(inverse)
            product = inverse - dot3(split_bf16(skew_ref[block]), parts)
            update = dot3(parts, split_bf16(product * scale))
            inverse_ref[block] = scale * (2.0 * inverse - update)

    def keep_going(carry):
        return carry[0, 0] < 0.97

    def scaled_step(carry):
        step(2.0 / (1.0 + carry))
        return 4.0 * carry / ((1.0 + carry) * (1.0 + carry))

    lax.while_loop(keep_going, scaled_step, least)
    step(jnp.ones((1, 1), jnp.float32))
    for block in range(count):
        inverse = inverse_ref[block]
        skew = skew_ref[block]
        rest = identity - inverse + jnp.dot(skew, inverse, precision=HIGH, preferred_element_type=jnp.float32)
        fixed = inverse + dot3(split_bf16(inverse), split_bf16(rest))
        rotation_ref[block] = 2.0 * fixed - identity

def cayley(tenant, oft_skew):
    count, order = oft_skew.shape[1], oft_skew.shape[2]
    return pl.pallas_call(
        cayley_kernel,
        out_shape=jax.ShapeDtypeStruct((count, order, order), jnp.float32),
        grid_spec=pltpu.PrefetchScalarGridSpec(
            num_scalar_prefetch=1,
            grid=(1,),
            in_specs=[pl.BlockSpec((1, count, order, order), lambda i, tenant: (tenant[0], 0, 0, 0))],
            out_specs=pl.BlockSpec((count, order, order), lambda i, tenant: (0, 0, 0)),
            scratch_shapes=[
                pltpu.VMEM((count, order, order), jnp.float32),
                pltpu.VMEM((count, order, order), jnp.float32),
            ],
        ),
        compiler_params=pltpu.CompilerParams(vmem_limit_bytes=60 << 20),
        cost_estimate=pl.CostEstimate(flops=20_000_000_000, bytes_accessed=2_000_000, transcendentals=0),
    )(tenant, oft_skew)


def rotate_kernel(full_width, tokens_ref, gain_ref, rotation_ref, *rest):
    sums_refs, turned_ref = rest[:-1], rest[-1]
    rows, order = tokens_ref.shape[0], rotation_ref.shape[1]
    sums = sums_refs[0][...]
    for sums_ref in sums_refs[1:]:
        sums = sums + sums_ref[...]
    sums = jnp.broadcast_to(sums, (rows, 2 * rows))
    lane = lax.broadcasted_iota(jnp.int32, sums.shape, 1)
    row = lax.broadcasted_iota(jnp.int32, sums.shape, 0)
    total = jnp.sum(jnp.where(lane == row, sums, 0.0), 1, keepdims=True)
    squares = jnp.sum(jnp.where(lane == row + rows, sums, 0.0), 1, keepdims=True)
    row_mean = total / full_width
    row_var = squares / full_width - row_mean * row_mean
    row_scale = lax.rsqrt(row_var + 1e-06)
    for block in range(rotation_ref.shape[0]):
        columns = pl.ds(block * order, order)
        floats = tokens_ref[:, columns].astype(jnp.float32)
        normed = (floats - row_mean) * row_scale * gain_ref[:, columns]
        turned = jnp.dot(
            normed, rotation_ref[block], precision=HIGH, preferred_element_type=jnp.float32
        )
        turned_ref[:, columns] = turned.astype(jnp.bfloat16)


def rotate(tokens, sums, gain, rotation, full_width):
    return pl.pallas_call(
        functools.partial(rotate_kernel, full_width),
        out_shape=jax.ShapeDtypeStruct(tokens.shape, jnp.bfloat16),
        cost_estimate=pl.CostEstimate(
            flops=600_000_000, bytes_accessed=1_000_000, transcendentals=0
        ),
    )(tokens, gain, rotation, *sums)


def head_norm(values_in, gain):
    width_count = values_in.shape[-1]
    row_mean = jnp.sum(values_in, -1, keepdims=True) / width_count
    row_var = jnp.sum(values_in * values_in, -1, keepdims=True) / width_count - row_mean * row_mean
    return (values_in - row_mean) * lax.rsqrt(row_var + 1e-06) * gain


def heads_kernel(sum_ref, far_ref, q_gain_ref, k_gain_ref, queries_ref, pair_ref):
    rows, head_dim = far_ref.shape[0], q_gain_ref.shape[-1]
    for head in range(2):
        columns = pl.ds(head * 3 * head_dim, 3 * head_dim)
        qkv = sum_ref[:rows, columns] + far_ref[:, columns].astype(jnp.float32)
        queries = head_norm(qkv[:, :head_dim], q_gain_ref[head])
        keys_normed = head_norm(qkv[:, head_dim : 2 * head_dim], k_gain_ref[head])
        queries_ref[head] = queries.astype(jnp.bfloat16)
        pair_ref[head, 0] = keys_normed.astype(jnp.bfloat16)
        pair_ref[head, 1] = qkv[:, 2 * head_dim :].astype(jnp.bfloat16)


def heads(total, far, q_gain, k_gain):
    rows = far.shape[0]
    head_dim = q_gain.shape[-1]
    return pl.pallas_call(
        heads_kernel,
        out_shape=(
            jax.ShapeDtypeStruct((2, rows, head_dim), jnp.bfloat16),
            jax.ShapeDtypeStruct((2, 2, rows, head_dim), jnp.bfloat16),
        ),
        cost_estimate=pl.CostEstimate(
            flops=10_000_000, bytes_accessed=2_000_000, transcendentals=0
        ),
    )(total, far, q_gain, k_gain)


def attention_kernel(queries_ref, pair_ref, other_ref, attended_ref):
    head_dim = queries_ref.shape[-1]
    for head in range(2):
        keys = jnp.concatenate([pair_ref[head, 0], other_ref[1 - head, 0]], 0)
        values = jnp.concatenate([pair_ref[head, 1], other_ref[1 - head, 1]], 0)
        scores = lax.dot_general(
            queries_ref[head], keys, (((1,), (1,)), ((), ())), preferred_element_type=jnp.float32
        ) / jnp.sqrt(jnp.float32(head_dim))
        expo = jnp.exp(scores - jnp.max(scores, -1, keepdims=True))
        weights = (expo / jnp.sum(expo, -1, keepdims=True)).astype(jnp.bfloat16)
        attended = jnp.dot(weights, values, preferred_element_type=jnp.float32)
        attended_ref[:, head * head_dim : (head + 1) * head_dim] = attended.astype(jnp.bfloat16)


def attention(queries, pair, other):
    heads_here, rows, head_dim = queries.shape
    return pl.pallas_call(
        attention_kernel,
        out_shape=jax.ShapeDtypeStruct((rows, heads_here * head_dim), jnp.bfloat16),
        cost_estimate=pl.CostEstimate(
            flops=40_000_000, bytes_accessed=1_000_000, transcendentals=70_000
        ),
    )(queries, pair, other)


def swap(value):
    return lax.ppermute(value, "core", [(0, 1), (1, 0)])


def shift(value, axis, distance):
    size = lax.axis_size(axis)
    return lax.ppermute(value, axis, [(i, (i + distance) % size) for i in range(size)])


def mirror(value, axis, mask):
    return lax.ppermute(value, axis, [(i, i ^ mask) for i in range(lax.axis_size(axis))])


def from_ahead(value, axis):
    size = lax.axis_size(axis)
    sent = {k: shift(value, axis, k) for k in FAR_FIRST}
    return [value] + [sent[size - k] for k in range(1, size)]


def sum_features(blocks, weights):
    size = len(blocks)
    partial = [matmul(blocks[k], weights).astype(jnp.bfloat16) for k in FAR_FIRST]
    sent = {k: shift(value, "x", k) for k, value in zip(FAR_FIRST, partial)}
    total = matmul(blocks[0], weights)
    for k in reversed(FAR_FIRST):
        total = total + sent[size - k].astype(jnp.float32)
    half = total.shape[0] // 2
    return total, shift(total[half:].astype(jnp.bfloat16), "zh", 1), partial


def share_rows(value):
    return from_ahead(jnp.concatenate([value, shift(value, "zh", 1)], 0), "x")


def matmul(left, right):
    return jnp.dot(left, right, preferred_element_type=jnp.float32)


def per_device(
    tokens,
    ln_gain,
    oft_skew,
    tenant_of_image,
    w_qkv,
    w_up,
    up_bias,
    q_gain,
    k_gain,
    w_out,
    w_down,
    down_bias,
):
    row_count, local_width = tokens.shape
    head_dim = w_qkv.shape[3]
    qkv_cols = 3 * head_dim
    across, along = lax.axis_size("zh"), lax.axis_size("x")
    group = across * along

    small_own = jnp.concatenate([up_bias[None], q_gain, k_gain], 1)
    small = jnp.stack([small_own, swap(small_own)])
    qkv_own = w_qkv.reshape(local_width, qkv_cols)
    out_own = w_out.reshape(head_dim, w_out.shape[2])
    qkv_both = jnp.concatenate([qkv_own, swap(qkv_own)], 1)
    up_other = swap(w_up)
    second = (jnp.concatenate([w_down, out_own, swap(out_own)], 0), swap(w_down))
    hidden_width = up_bias.shape[0]
    bias = small[:, 0, :hidden_width]
    q_gains = small[:, :, hidden_width : hidden_width + head_dim]
    k_gains = small[:, :, hidden_width + head_dim :]

    floats = tokens.astype(jnp.float32)
    row_sums = jnp.concatenate([jnp.sum(floats, 1), jnp.sum(floats * floats, 1)])[None]
    pairs = [divmod(step, along) for step in range(group)]
    all_sums = [row_sums] + [
        lax.ppermute(
            row_sums,
            GY,
            [
                (z * along + x, (z + dz) % across * along + (x + dx) % along)
                for z in range(across)
                for x in range(along)
            ],
        )
        for dz, dx in pairs[1:]
    ]

    image_index = lax.axis_index(GX) * row_count // PATCHES
    tenant = lax.dynamic_slice_in_dim(tenant_of_image, image_index, 1, 0)
    rotation = cayley(tenant, oft_skew)
    turned = rotate(tokens, all_sums, ln_gain[None], rotation, local_width * group)

    layers, lines = lax.axis_size("zl"), lax.axis_size("y")
    here, side = lax.axis_index("x"), lax.axis_index("zh")
    layer, line = lax.axis_index("zl"), lax.axis_index("y")
    column = jnp.stack([turned] + [mirror(turned, "zl", mask) for mask in range(1, layers)])
    gathered = jnp.stack(from_ahead(column, "y"))

    def image_rows(z, x):
        image = z * along + x
        its_layer, first_line = image // 2, image % 2 * 2
        return [
            gathered[lax.rem(lines + first_line + step - line, lines), its_layer ^ layer]
            for step in range(2)
        ]

    blocks = []
    for k in range(along):
        x = lax.rem(here + k, along)
        blocks.append(jnp.concatenate(image_rows(side, x) + image_rows(1 - side, x), 0))

    total, far, partial = sum_features(blocks, qkv_both)
    queries, pair = heads(total, far, q_gains, k_gains)
    attended = attention(queries, pair, swap(pair))
    hidden = []
    for core, weights in enumerate((w_up, up_other)):
        blocks = lax.optimization_barrier((blocks, partial))[0]
        total, far, partial = sum_features(blocks, weights)
        up_pre = total[: far.shape[0]] + far.astype(jnp.float32) + bias[core]
        hidden.append(jax.nn.gelu(up_pre, approximate=False).astype(jnp.bfloat16))

    first_rows = share_rows(jnp.concatenate([hidden[0], attended], 1))
    last_rows = share_rows(hidden[1])
    parts = [
        (matmul(first_part, second[0]) + matmul(last_part, second[1])).astype(jnp.bfloat16)
        for first_part, last_part in zip(first_rows, last_rows)
    ]
    parts = jnp.stack(parts).reshape(along, across, 2, row_count, local_width)

    def owned_by(its_layer, its_line):
        image = its_layer * 2 + its_line // 2
        step = lax.rem(along + image % along - here, along)
        return parts[step, image // along ^ side, its_line % 2]

    outgoing = [
        jnp.stack([owned_by(layer ^ mask, lax.rem(line + k, lines)) for mask in range(layers)])
        for k in range(lines)
    ]
    sent = {k: shift(outgoing[k], "y", k) for k in FAR_FIRST}
    total = outgoing[0].astype(jnp.float32)
    for k in FAR_FIRST:
        total = total + sent[k].astype(jnp.float32)
    mixed = total[0]
    for mask in range(1, layers):
        mixed = mixed + mirror(total[mask].astype(jnp.bfloat16), "zl", mask).astype(jnp.float32)
    return (floats + mixed + down_bias).astype(jnp.bfloat16)


def solution(mesh):
    names = tuple(name for name, _ in AXES)
    sizes = tuple(size for _, size in AXES)
    fine_mesh = Mesh(mesh.devices.reshape(sizes), names)
    in_specs = (
        P(GX, GY),
        P(GY),
        P(None, GY, None, None),
        P(),
        P(GY, GX, None, None),
        P(GY, GX),
        P(GX),
        P(GX, None),
        P(GX, None),
        P(GX, None, GY),
        P(GX, GY),
        P(GY),
    )
    return jax.shard_map(
        per_device, mesh=fine_mesh, in_specs=in_specs, out_specs=P(GX, GY), check_vma=False
    )
```

```python
import functools

import jax
import jax.numpy as jnp
from jax import lax
from jax.experimental import pallas as pl
from jax.experimental.pallas import tpu as pltpu
from jax.sharding import Mesh
from jax.sharding import PartitionSpec as P

PATCHES = 256
HIGH = lax.Precision.HIGHEST
AXES = (("zl", 4), ("y", 4), ("core", 2), ("zh", 2), ("x", 4))
GX = ("zl", "y", "core")
GY = ("zh", "x")
FAR_FIRST = (2, 1, 3)


def split_bf16(value):
    high = value.astype(jnp.bfloat16)
    low = (value - high.astype(jnp.float32)).astype(jnp.bfloat16)
    return high, low

def dot3(left, right):
    left_high, left_low = left
    right_high, right_low = right
    return jnp.dot(
        jnp.concatenate([left_high, left_high, left_low], 1),
        jnp.concatenate([right_high, right_low, right_high], 0),
        preferred_element_type=jnp.float32,
    )

def cayley_kernel(tenant_ref, raw_ref, rotation_ref, skew_ref, inverse_ref):
    count, order = raw_ref.shape[1], raw_ref.shape[2]
    identity = (
        lax.broadcasted_iota(jnp.int32, (order, order), 0)
        == lax.broadcasted_iota(jnp.int32, (order, order), 1)
    ).astype(jnp.float32)
    bounds = []
    for block in range(count):
        raw = raw_ref[0, block]
        skew = 0.5 * (raw.T - raw)
        parts = split_bf16(skew)
        skew_ref[block] = skew
        gram = identity - dot3(parts, parts)
        bounds.append(1.001 * jnp.sqrt(0.5 * jnp.sum(gram * gram, keepdims=True)))
        inverse_ref[block] = gram
    top = functools.reduce(jnp.maximum, bounds)
    least = 1.0 / top
    scale = 2.0 * top / (1.0 + top)
    for block in range(count):
        start = (identity + skew_ref[block]) * least
        ratio = inverse_ref[block] * (least * scale)
        update = dot3(split_bf16(start), split_bf16(ratio))
        inverse_ref[block] = scale * (2.0 * start - update)
    least = 4.0 * top / ((1.0 + top) * (1.0 + top))

    def step(scale):
        for block in range(count):
            inverse = inverse_ref[block]
            parts = split_bf16(inverse)
            product = inverse - dot3(split_bf16(skew_ref[block]), parts)
            update = dot3(parts, split_bf16(product * scale))
            inverse_ref[block] = scale * (2.0 * inverse - update)

    def keep_going(carry):
        return carry[0, 0] < 0.97

    def scaled_step(carry):
        step(2.0 / (1.0 + carry))
        return 4.0 * carry / ((1.0 + carry) * (1.0 + carry))

    lax.while_loop(keep_going, scaled_step, least)
    step(jnp.ones((1, 1), jnp.float32))
    for block in range(count):
        inverse = inverse_ref[block]
        skew = skew_ref[block]
        rest = identity - inverse + jnp.dot(skew, inverse, precision=HIGH, preferred_element_type=jnp.float32)
        fixed = inverse + dot3(split_bf16(inverse), split_bf16(rest))
        rotation_ref[block] = 2.0 * fixed - identity

def cayley(tenant, oft_skew):
    count, order = oft_skew.shape[1], oft_skew.shape[2]
    return pl.pallas_call(
        cayley_kernel,
        out_shape=jax.ShapeDtypeStruct((count, order, order), jnp.float32),
        grid_spec=pltpu.PrefetchScalarGridSpec(
            num_scalar_prefetch=1,
            grid=(1,),
            in_specs=[pl.BlockSpec((1, count, order, order), lambda i, tenant: (tenant[0], 0, 0, 0))],
            out_specs=pl.BlockSpec((count, order, order), lambda i, tenant: (0, 0, 0)),
            scratch_shapes=[
                pltpu.VMEM((count, order, order), jnp.float32),
                pltpu.VMEM((count, order, order), jnp.float32),
            ],
        ),
        compiler_params=pltpu.CompilerParams(vmem_limit_bytes=60 << 20),
        cost_estimate=pl.CostEstimate(flops=20_000_000_000, bytes_accessed=2_000_000, transcendentals=0),
    )(tenant, oft_skew)


def rotate_kernel(full_width, tokens_ref, gain_ref, rotation_ref, sums_ref, turned_ref):
    rows, order = tokens_ref.shape[0], rotation_ref.shape[1]
    sums = jnp.broadcast_to(jnp.sum(sums_ref[...], 0), (rows, 2 * rows))
    lane = lax.broadcasted_iota(jnp.int32, sums.shape, 1)
    row = lax.broadcasted_iota(jnp.int32, sums.shape, 0)
    total = jnp.sum(jnp.where(lane == row, sums, 0.0), 1, keepdims=True)
    squares = jnp.sum(jnp.where(lane == row + rows, sums, 0.0), 1, keepdims=True)
    row_mean = total / full_width
    row_var = squares / full_width - row_mean * row_mean
    row_scale = lax.rsqrt(row_var + 1e-06)
    for block in range(rotation_ref.shape[0]):
        columns = pl.ds(block * order, order)
        floats = tokens_ref[:, columns].astype(jnp.float32)
        normed = (floats - row_mean) * row_scale * gain_ref[:, columns]
        turned = jnp.dot(
            normed, rotation_ref[block], precision=HIGH, preferred_element_type=jnp.float32
        )
        turned_ref[:, columns] = turned.astype(jnp.bfloat16)


def rotate(tokens, sums, gain, rotation, full_width):
    return pl.pallas_call(
        functools.partial(rotate_kernel, full_width),
        out_shape=jax.ShapeDtypeStruct(tokens.shape, jnp.bfloat16),
        cost_estimate=pl.CostEstimate(
            flops=600_000_000, bytes_accessed=1_000_000, transcendentals=0
        ),
    )(tokens, gain, rotation, sums)


def head_norm(values_in, gain):
    width_count = values_in.shape[-1]
    row_mean = jnp.sum(values_in, -1, keepdims=True) / width_count
    row_var = jnp.sum(values_in * values_in, -1, keepdims=True) / width_count - row_mean * row_mean
    return (values_in - row_mean) * lax.rsqrt(row_var + 1e-06) * gain


def heads_kernel(sum_ref, far_ref, q_gain_ref, k_gain_ref, queries_ref, pair_ref):
    head_dim = q_gain_ref.shape[-1]
    for head in range(2):
        columns = pl.ds(head * 3 * head_dim, 3 * head_dim)
        qkv = sum_ref[:, columns] + far_ref[:, columns].astype(jnp.float32)
        queries = head_norm(qkv[:, :head_dim], q_gain_ref[head])
        keys_normed = head_norm(qkv[:, head_dim : 2 * head_dim], k_gain_ref[head])
        queries_ref[head] = queries.astype(jnp.bfloat16)
        pair_ref[head, 0] = keys_normed.astype(jnp.bfloat16)
        pair_ref[head, 1] = qkv[:, 2 * head_dim :].astype(jnp.bfloat16)


def heads(total, far, q_gain, k_gain):
    rows = far.shape[0]
    head_dim = q_gain.shape[-1]
    return pl.pallas_call(
        heads_kernel,
        out_shape=(
            jax.ShapeDtypeStruct((2, rows, head_dim), jnp.bfloat16),
            jax.ShapeDtypeStruct((2, 2, rows, head_dim), jnp.bfloat16),
        ),
        cost_estimate=pl.CostEstimate(
            flops=10_000_000, bytes_accessed=2_000_000, transcendentals=0
        ),
    )(total, far, q_gain, k_gain)


def attention_kernel(queries_ref, pair_ref, other_ref, attended_ref):
    head_dim = queries_ref.shape[-1]
    for head in range(2):
        keys = jnp.concatenate([pair_ref[head, 0], other_ref[1 - head, 0]], 0)
        values = jnp.concatenate([pair_ref[head, 1], other_ref[1 - head, 1]], 0)
        scores = lax.dot_general(
            queries_ref[head], keys, (((1,), (1,)), ((), ())), preferred_element_type=jnp.float32
        ) / jnp.sqrt(jnp.float32(head_dim))
        expo = jnp.exp(scores - jnp.max(scores, -1, keepdims=True))
        weights = (expo / jnp.sum(expo, -1, keepdims=True)).astype(jnp.bfloat16)
        attended = jnp.dot(weights, values, preferred_element_type=jnp.float32)
        attended_ref[:, head * head_dim : (head + 1) * head_dim] = attended.astype(jnp.bfloat16)


def attention(queries, pair, other):
    heads_here, rows, head_dim = queries.shape
    return pl.pallas_call(
        attention_kernel,
        out_shape=jax.ShapeDtypeStruct((rows, heads_here * head_dim), jnp.bfloat16),
        cost_estimate=pl.CostEstimate(
            flops=40_000_000, bytes_accessed=1_000_000, transcendentals=70_000
        ),
    )(queries, pair, other)


def reorder_kernel(source, blocks_ref, ordered_ref):
    for place in range(ordered_ref.shape[0]):
        ordered_ref[place] = blocks_ref[source(place)]


def reorder(blocks, source):
    return pl.pallas_call(
        functools.partial(reorder_kernel, source),
        out_shape=jax.ShapeDtypeStruct(blocks.shape, blocks.dtype),
        cost_estimate=pl.CostEstimate(flops=0, bytes_accessed=3_000_000, transcendentals=0),
    )(blocks)


def row_source(place):
    step, half, second = place // 4, place // 2 % 2, place % 2
    x = lax.rem(lax.axis_index("x") + step, 4)
    image = (lax.axis_index("zh") ^ half) * 4 + x
    line = lax.rem(4 + image % 2 * 2 + second - lax.axis_index("y"), 4)
    return line * 4 + (image // 2 ^ lax.axis_index("zl"))


def owner_source(place):
    line = lax.rem(lax.axis_index("y") + place // 4, 4)
    image = place % 4 * 2 + line // 2
    step = lax.rem(4 + image % 4 - lax.axis_index("x"), 4)
    return (step ^ step // 2) * 4 + (image // 4 ^ lax.axis_index("zh")) * 2 + line % 2


def swap(value):
    return lax.ppermute(value, "core", [(0, 1), (1, 0)])


def shift(value, axis, distance):
    size = lax.axis_size(axis)
    return lax.ppermute(value, axis, [(i, (i + distance) % size) for i in range(size)])


def mirror(value, axis, mask):
    return lax.ppermute(value, axis, [(i, i ^ mask) for i in range(lax.axis_size(axis))])


def from_ahead(value, axis):
    size = lax.axis_size(axis)
    sent = {k: shift(value, axis, k) for k in FAR_FIRST}
    return [value] + [sent[size - k] for k in range(1, size)]


def sum_features(rows, weights, after):
    product = matmul(rows, weights).reshape(4, 2, rows.shape[0] // 8, weights.shape[1])
    two_steps = lax.optimization_barrier((product[2].astype(jnp.bfloat16), after[:1]))[0]
    first = (shift(two_steps[0], "x", 1), shift(two_steps[1], "x", -1))
    ahead = product[1] + jnp.stack([first[0].astype(jnp.float32), jnp.zeros_like(product[1, 1])])
    behind = product[3] + jnp.stack([jnp.zeros_like(product[3, 0]), first[1].astype(jnp.float32)])
    ahead, behind = ahead.astype(jnp.bfloat16), behind.astype(jnp.bfloat16)
    ahead, behind = lax.optimization_barrier(((ahead, behind), after[1:]))[0]
    ahead, behind = shift(ahead, "x", 1), shift(behind, "x", -1)
    total = product[0] + ahead.astype(jnp.float32) + behind.astype(jnp.float32)
    return total[0], shift(total[1].astype(jnp.bfloat16), "zh", 1), (first, (ahead, behind))


def share_rows(value):
    half = value.shape[0]
    both = jnp.concatenate([value, shift(value, "zh", 1)], 0)
    behind, ahead = shift(both, "x", 1), shift(both, "x", -1)
    across = [shift(behind[:half], "x", 1), shift(ahead[half:], "x", -1)]
    return jnp.concatenate([both, ahead, behind], 0), jnp.concatenate(across, 0)


def matmul(left, right):
    return jnp.dot(left, right, preferred_element_type=jnp.float32)


def per_device(
    tokens,
    ln_gain,
    oft_skew,
    tenant_of_image,
    w_qkv,
    w_up,
    up_bias,
    q_gain,
    k_gain,
    w_out,
    w_down,
    down_bias,
):
    row_count, local_width = tokens.shape
    head_dim = w_qkv.shape[3]
    qkv_cols = 3 * head_dim
    across, along = lax.axis_size("zh"), lax.axis_size("x")
    group = across * along

    small_own = jnp.concatenate([up_bias[None], q_gain, k_gain], 1)
    small = jnp.stack([small_own, swap(small_own)])
    qkv_own = w_qkv.reshape(local_width, qkv_cols)
    out_own = w_out.reshape(head_dim, w_out.shape[2])
    first_both = jnp.concatenate([qkv_own, swap(qkv_own), w_up], 1)
    far_side = swap(jnp.concatenate([w_up, w_down, out_own], 0))
    hidden_width = up_bias.shape[0]
    bias = small[:, 0, :hidden_width]
    q_gains = small[:, :, hidden_width : hidden_width + head_dim]
    k_gains = small[:, :, hidden_width + head_dim :]

    floats = tokens.astype(jnp.float32)
    row_sums = jnp.concatenate([jnp.sum(floats, 1), jnp.sum(floats * floats, 1)])[None]
    row_sums = jnp.broadcast_to(row_sums[None], (group, 1, 2 * row_count))
    row_sums = lax.all_to_all(row_sums, GY, 0, 0, tiled=True)

    image_index = lax.axis_index(GX) * row_count // PATCHES
    tenant = lax.dynamic_slice_in_dim(tenant_of_image, image_index, 1, 0)
    rotation = cayley(tenant, oft_skew)
    turned = rotate(tokens, row_sums, ln_gain[None], rotation, local_width * group)

    layers, lines = lax.axis_size("zl"), lax.axis_size("y")
    column = jnp.stack([turned] + [mirror(turned, "zl", mask) for mask in range(1, layers)])
    gathered = jnp.concatenate(from_ahead(column, "y"), 0)
    rows = reorder(gathered, row_source).reshape(layers * lines * row_count, local_width)
    rows, far_side = lax.optimization_barrier((rows, far_side))
    up_other, second_other = far_side[:local_width], far_side[local_width:]
    second = jnp.concatenate([w_down, second_other[:-head_dim], out_own, second_other[-head_dim:]], 0)

    total, far, came = sum_features(rows, first_both, ())
    queries, pair = heads(total, far, q_gains, k_gains)
    other = swap(pair)
    last_total, last_far, _ = sum_features(rows, up_other, came)
    attended = attention(queries, pair, other)
    up_pre = (
        total[:, 2 * qkv_cols :] + far[:, 2 * qkv_cols :].astype(jnp.float32) + bias[0],
        last_total + last_far.astype(jnp.float32) + bias[1],
    )
    hidden = [jax.nn.gelu(value, approximate=False).astype(jnp.bfloat16) for value in up_pre]

    near, far = share_rows(jnp.concatenate([*hidden, attended], 1))
    parts = [matmul(near, second).astype(jnp.bfloat16), matmul(far, second).astype(jnp.bfloat16)]
    parts = jnp.concatenate(parts, 0)
    outgoing = reorder(parts.reshape(layers * lines, row_count, local_width), owner_source)
    outgoing = outgoing.reshape(lines, layers, row_count, local_width)
    sent = {k: shift(outgoing[k], "y", k) for k in FAR_FIRST}
    total = outgoing[0].astype(jnp.float32)
    for k in FAR_FIRST:
        total = total + sent[k].astype(jnp.float32)
    returned = lax.all_to_all(total.astype(jnp.bfloat16), "zl", 0, 0, tiled=True)
    mixed = jnp.sum(returned.astype(jnp.float32), 0)
    return (floats + mixed + down_bias).astype(jnp.bfloat16)


def solution(mesh):
    names = tuple(name for name, _ in AXES)
    sizes = tuple(size for _, size in AXES)
    fine_mesh = Mesh(mesh.devices.reshape(sizes), names)
    in_specs = (
        P(GX, GY),
        P(GY),
        P(None, GY, None, None),
        P(),
        P(GY, GX, None, None),
        P(GY, GX),
        P(GX),
        P(GX, None),
        P(GX, None),
        P(GX, None, GY),
        P(GX, GY),
        P(GY),
    )
    return jax.shard_map(
        per_device, mesh=fine_mesh, in_specs=in_specs, out_specs=P(GX, GY), check_vma=False
    )
```

```python
import functools

import jax
import jax.numpy as jnp
from jax import lax
from jax.experimental import pallas as pl
from jax.experimental.pallas import tpu as pltpu
from jax.sharding import Mesh
from jax.sharding import PartitionSpec as P

PATCHES = 256
HIGH = lax.Precision.HIGHEST
AXES = (("zl", 4), ("y", 4), ("core", 2), ("zh", 2), ("x", 4))
GX = ("zl", "y", "core")
GY = ("zh", "x")
FAR_FIRST = (2, 1, 3)


def split_bf16(value):
    high = value.astype(jnp.bfloat16)
    low = (value - high.astype(jnp.float32)).astype(jnp.bfloat16)
    return high, low

def dot3(left, right):
    left_high, left_low = left
    right_high, right_low = right
    return jnp.dot(
        jnp.concatenate([left_high, left_high, left_low], 1),
        jnp.concatenate([right_high, right_low, right_high], 0),
        preferred_element_type=jnp.float32,
    )

def cayley_kernel(tenant_ref, raw_ref, rotation_ref, skew_ref, inverse_ref):
    count, order = raw_ref.shape[1], raw_ref.shape[2]
    identity = (
        lax.broadcasted_iota(jnp.int32, (order, order), 0)
        == lax.broadcasted_iota(jnp.int32, (order, order), 1)
    ).astype(jnp.float32)
    bounds = []
    for block in range(count):
        raw = raw_ref[0, block]
        skew = 0.5 * (raw.T - raw)
        parts = split_bf16(skew)
        skew_ref[block] = skew
        gram = identity - dot3(parts, parts)
        bounds.append(1.001 * jnp.sqrt(0.5 * jnp.sum(gram * gram, keepdims=True)))
        inverse_ref[block] = gram
    top = functools.reduce(jnp.maximum, bounds)
    least = 1.0 / top
    scale = 2.0 * top / (1.0 + top)
    for block in range(count):
        start = (identity + skew_ref[block]) * least
        ratio = inverse_ref[block] * (least * scale)
        update = dot3(split_bf16(start), split_bf16(ratio))
        inverse_ref[block] = scale * (2.0 * start - update)
    least = 4.0 * top / ((1.0 + top) * (1.0 + top))

    def step(scale):
        for block in range(count):
            inverse = inverse_ref[block]
            parts = split_bf16(inverse)
            product = inverse - dot3(split_bf16(skew_ref[block]), parts)
            update = dot3(parts, split_bf16(product * scale))
            inverse_ref[block] = scale * (2.0 * inverse - update)

    def keep_going(carry):
        return carry[0, 0] < 0.9995

    def scaled_step(carry):
        step(2.0 / (1.0 + carry))
        return 4.0 * carry / ((1.0 + carry) * (1.0 + carry))

    lax.while_loop(keep_going, scaled_step, least)
    for block in range(count):
        inverse = inverse_ref[block]
        skew = skew_ref[block]
        rest = identity - inverse + jnp.dot(skew, inverse, precision=HIGH, preferred_element_type=jnp.float32)
        fixed = inverse + dot3(split_bf16(inverse), split_bf16(rest))
        rotation_ref[block] = 2.0 * fixed - identity

def cayley(tenant, oft_skew):
    count, order = oft_skew.shape[1], oft_skew.shape[2]
    return pl.pallas_call(
        cayley_kernel,
        out_shape=jax.ShapeDtypeStruct((count, order, order), jnp.float32),
        grid_spec=pltpu.PrefetchScalarGridSpec(
            num_scalar_prefetch=1,
            grid=(1,),
            in_specs=[pl.BlockSpec((1, count, order, order), lambda i, tenant: (tenant[0], 0, 0, 0))],
            out_specs=pl.BlockSpec((count, order, order), lambda i, tenant: (0, 0, 0)),
            scratch_shapes=[
                pltpu.VMEM((count, order, order), jnp.float32),
                pltpu.VMEM((count, order, order), jnp.float32),
            ],
        ),
        compiler_params=pltpu.CompilerParams(vmem_limit_bytes=60 << 20),
        cost_estimate=pl.CostEstimate(flops=20_000_000_000, bytes_accessed=2_000_000, transcendentals=0),
    )(tenant, oft_skew)


def rotate_kernel(full_width, tokens_ref, gain_ref, rotation_ref, sums_ref, turned_ref):
    rows, order = tokens_ref.shape[0], rotation_ref.shape[1]
    sums = jnp.broadcast_to(jnp.sum(sums_ref[...], 0), (rows, 2 * rows))
    lane = lax.broadcasted_iota(jnp.int32, sums.shape, 1)
    row = lax.broadcasted_iota(jnp.int32, sums.shape, 0)
    total = jnp.sum(jnp.where(lane == row, sums, 0.0), 1, keepdims=True)
    squares = jnp.sum(jnp.where(lane == row + rows, sums, 0.0), 1, keepdims=True)
    row_mean = total / full_width
    row_var = squares / full_width - row_mean * row_mean
    row_scale = lax.rsqrt(row_var + 1e-06)
    for block in range(rotation_ref.shape[0]):
        columns = pl.ds(block * order, order)
        floats = tokens_ref[:, columns].astype(jnp.float32)
        normed = (floats - row_mean) * row_scale * gain_ref[:, columns]
        turned = jnp.dot(
            normed, rotation_ref[block], precision=HIGH, preferred_element_type=jnp.float32
        )
        turned_ref[:, columns] = turned.astype(jnp.bfloat16)


def rotate(tokens, sums, gain, rotation, full_width):
    return pl.pallas_call(
        functools.partial(rotate_kernel, full_width),
        out_shape=jax.ShapeDtypeStruct(tokens.shape, jnp.bfloat16),
        cost_estimate=pl.CostEstimate(
            flops=600_000_000, bytes_accessed=1_000_000, transcendentals=0
        ),
    )(tokens, gain, rotation, sums)


def head_norm(values_in, gain):
    width_count = values_in.shape[-1]
    row_mean = jnp.sum(values_in, -1, keepdims=True) / width_count
    row_var = jnp.sum(values_in * values_in, -1, keepdims=True) / width_count - row_mean * row_mean
    return (values_in - row_mean) * lax.rsqrt(row_var + 1e-06) * gain


def heads_kernel(sum_ref, far_ref, q_gain_ref, k_gain_ref, queries_ref, pair_ref):
    head_dim = q_gain_ref.shape[-1]
    for head in range(2):
        columns = pl.ds(head * 3 * head_dim, 3 * head_dim)
        qkv = sum_ref[:, columns] + far_ref[:, columns].astype(jnp.float32)
        queries = head_norm(qkv[:, :head_dim], q_gain_ref[head])
        keys_normed = head_norm(qkv[:, head_dim : 2 * head_dim], k_gain_ref[head])
        queries_ref[head] = queries.astype(jnp.bfloat16)
        pair_ref[head, 0] = keys_normed.astype(jnp.bfloat16)
        pair_ref[head, 1] = qkv[:, 2 * head_dim :].astype(jnp.bfloat16)


def heads(total, far, q_gain, k_gain):
    rows, columns = far.shape
    head_dim = q_gain.shape[-1]
    return pl.pallas_call(
        heads_kernel,
        out_shape=(
            jax.ShapeDtypeStruct((2, rows, head_dim), jnp.bfloat16),
            jax.ShapeDtypeStruct((2, 2, rows, head_dim), jnp.bfloat16),
        ),
        grid=(1,),
        in_specs=[
            pl.BlockSpec((rows, columns), lambda i: (0, 0)),
            pl.BlockSpec((rows, columns), lambda i: (0, 0)),
            pl.BlockSpec((2, 1, head_dim), lambda i: (0, 0, 0)),
            pl.BlockSpec((2, 1, head_dim), lambda i: (0, 0, 0)),
        ],
        out_specs=(
            pl.BlockSpec((2, rows, head_dim), lambda i: (0, 0, 0)),
            pl.BlockSpec((2, 2, rows, head_dim), lambda i: (0, 0, 0, 0)),
        ),
        cost_estimate=pl.CostEstimate(
            flops=10_000_000, bytes_accessed=2_000_000, transcendentals=0
        ),
    )(total, far, q_gain, k_gain)


def attention_kernel(queries_ref, pair_ref, other_ref, attended_ref):
    head_dim = queries_ref.shape[-1]
    for head in range(2):
        keys = jnp.concatenate([pair_ref[head, 0], other_ref[1 - head, 0]], 0)
        values = jnp.concatenate([pair_ref[head, 1], other_ref[1 - head, 1]], 0)
        scores = lax.dot_general(
            queries_ref[head], keys, (((1,), (1,)), ((), ())), preferred_element_type=jnp.float32
        ) / jnp.sqrt(jnp.float32(head_dim))
        expo = jnp.exp(scores - jnp.max(scores, -1, keepdims=True))
        weights = (expo / jnp.sum(expo, -1, keepdims=True)).astype(jnp.bfloat16)
        attended = jnp.dot(weights, values, preferred_element_type=jnp.float32)
        attended_ref[:, head * head_dim : (head + 1) * head_dim] = attended.astype(jnp.bfloat16)


def attention(queries, pair, other):
    heads_here, rows, head_dim = queries.shape
    return pl.pallas_call(
        attention_kernel,
        out_shape=jax.ShapeDtypeStruct((rows, heads_here * head_dim), jnp.bfloat16),
        cost_estimate=pl.CostEstimate(
            flops=40_000_000, bytes_accessed=1_000_000, transcendentals=70_000
        ),
    )(queries, pair, other)


def reorder_kernel(source, given, *refs):
    blocks_refs, ordered_refs, held_ref = refs[:given], refs[given:-1], refs[-1]
    at = 0
    for blocks_ref in blocks_refs:
        held_ref[at : at + blocks_ref.shape[0]] = blocks_ref[...]
        at += blocks_ref.shape[0]
    place = 0
    for ordered_ref in ordered_refs:
        for row in range(ordered_ref.shape[0]):
            ordered_ref[row] = held_ref[source(place)]
            place += 1


def reorder(parts, source, pieces):
    count = sum(part.shape[0] for part in parts)
    block = parts[0].shape[1:]
    piece = jax.ShapeDtypeStruct((count // pieces, *block), parts[0].dtype)
    return pl.pallas_call(
        functools.partial(reorder_kernel, source, len(parts)),
        out_shape=(piece,) * pieces,
        scratch_shapes=[pltpu.VMEM((count, *block), parts[0].dtype)],
        cost_estimate=pl.CostEstimate(flops=0, bytes_accessed=3_000_000, transcendentals=0),
    )(*parts)


def row_source(place):
    half, step, second = 1 - place // 8, place // 2 % 4, place % 2
    x = lax.rem(lax.axis_index("x") + step, 4)
    image = (lax.axis_index("zh") ^ half) * 4 + x
    line = lax.rem(4 + image % 2 * 2 + second - lax.axis_index("y"), 4)
    return line * 4 + (image // 2 ^ lax.axis_index("zl"))


def owner_source(place):
    line = lax.rem(lax.axis_index("y") + place // 4, 4)
    image = place % 4 * 2 + line // 2
    step = lax.rem(4 + image % 4 - lax.axis_index("x"), 4)
    return (image // 4 ^ lax.axis_index("zh")) * 8 + (step ^ step // 2) * 2 + line % 2


def swap(value):
    return lax.ppermute(value, "core", [(0, 1), (1, 0)])


def shift(value, axis, distance):
    size = lax.axis_size(axis)
    return lax.ppermute(value, axis, [(i, (i + distance) % size) for i in range(size)])


def mirror(value, axis, mask):
    return lax.ppermute(value, axis, [(i, i ^ mask) for i in range(lax.axis_size(axis))])


def from_ahead(value, axis):
    size = lax.axis_size(axis)
    sent = {k: shift(value, axis, k) for k in FAR_FIRST}
    return [value] + [sent[size - k] for k in range(1, size)]


def products_kernel(rows_ref, own_ref, other_ref, up_ref, up_far_ref, here, ahead, behind, low, high, weights):
    step = pl.program_id(0)
    for first, qkv_ref in enumerate((own_ref, other_ref)):

        @pl.when(step == first)
        def _(qkv_ref=qkv_ref):
            weights[...] = jnp.concatenate([qkv_ref[part] for part in range(3)], 1)

    tiles = (pl.num_programs(0) - 2) // 2

    @pl.when(jnp.logical_and(step >= 2, step < 2 + tiles))
    def _():
        weights[...] = up_ref[...]

    @pl.when(step >= 2 + tiles)
    def _():
        weights[...] = up_far_ref[...]

    product = jnp.dot(rows_ref[...], weights[...], preferred_element_type=jnp.float32)
    count, half = here.shape[0], low.shape[0]
    here[...] = product[:count]
    ahead[...] = product[count : 2 * count]
    two_steps = product[2 * count : 3 * count].astype(jnp.bfloat16)
    low[...] = two_steps[:half]
    high[...] = two_steps[half:]
    behind[...] = product[3 * count :]


def products(rows, qkv_own, qkv_other, up_own, far_side):
    row_count, depth = rows.shape
    parts, _, head_dim = qkv_own.shape
    tile = parts * head_dim
    tiles = up_own.shape[1] // tile
    columns = (2 + 2 * tiles) * tile
    count = row_count // 4
    whole = pl.BlockSpec((parts, depth, head_dim), lambda i: (0, 0, 0))
    return pl.pallas_call(
        products_kernel,
        out_shape=(jax.ShapeDtypeStruct((count, columns), jnp.float32),) * 3
        + (jax.ShapeDtypeStruct((count // 2, columns), jnp.bfloat16),) * 2,
        grid=(2 + 2 * tiles,),
        in_specs=[
            pl.BlockSpec((row_count, depth), lambda i: (0, 0)),
            whole,
            whole,
            pl.BlockSpec((depth, tile), lambda i: (0, jnp.clip(i - 2, 0, tiles - 1))),
            pl.BlockSpec((depth, tile), lambda i: (0, jnp.clip(i - 2 - tiles, 0, tiles - 1))),
        ],
        out_specs=(pl.BlockSpec((count, tile), lambda i: (0, i)),) * 3
        + (pl.BlockSpec((count // 2, tile), lambda i: (0, i)),) * 2,
        scratch_shapes=[pltpu.VMEM((depth, tile), jnp.bfloat16)],
        cost_estimate=pl.CostEstimate(
            flops=2 * row_count * depth * columns, bytes_accessed=8_000_000, transcendentals=0
        ),
    )(rows, qkv_own, qkv_other, up_own, far_side)


def sum_along_x(rows, weights, after):
    here, ahead, behind, low, high = products(rows, *weights)
    half = low.shape[0]
    low, high = lax.optimization_barrier(((low, high), after[:1]))[0]
    first = (shift(low, "x", 1), shift(high, "x", -1))
    ahead = jnp.concatenate([ahead[:half] + first[0].astype(jnp.float32), ahead[half:]], 0)
    behind = jnp.concatenate([behind[:half], behind[half:] + first[1].astype(jnp.float32)], 0)
    ahead, behind = ahead.astype(jnp.bfloat16), behind.astype(jnp.bfloat16)
    ahead, behind = lax.optimization_barrier(((ahead, behind), after[1:]))[0]
    ahead, behind = shift(ahead, "x", 1), shift(behind, "x", -1)
    return here + ahead.astype(jnp.float32) + behind.astype(jnp.float32), (first, (ahead, behind))


def share_along_x(value):
    half = value.shape[0] // 2
    behind, ahead = shift(value, "x", 1), shift(value, "x", -1)
    across = [shift(behind[:half], "x", 1), shift(ahead[half:], "x", -1)]
    return jnp.concatenate([value, ahead, behind], 0), jnp.concatenate(across, 0)


def matmul(left, right):
    return jnp.dot(left, right, preferred_element_type=jnp.float32)


def per_device(
    tokens,
    ln_gain,
    oft_skew,
    tenant_of_image,
    w_qkv,
    w_up,
    up_bias,
    q_gain,
    k_gain,
    w_out,
    w_down,
    down_bias,
):
    row_count, local_width = tokens.shape
    head_dim = w_qkv.shape[3]
    qkv_cols = 3 * head_dim
    across, along = lax.axis_size("zh"), lax.axis_size("x")
    group = across * along

    hidden_width = up_bias.shape[0]
    small_own = jnp.concatenate([up_bias[None], q_gain, k_gain], 1)
    small = jnp.stack([small_own, swap(small_own)])
    bias = small[:, 0, :hidden_width].reshape(2 * hidden_width)
    q_gains = small[:, :, hidden_width : hidden_width + head_dim]
    k_gains = small[:, :, hidden_width + head_dim :]

    floats = tokens.astype(jnp.float32)
    row_sums = jnp.concatenate([jnp.sum(floats, 1), jnp.sum(floats * floats, 1)])[None]
    row_sums = jnp.broadcast_to(row_sums[None], (group, 1, 2 * row_count))
    row_sums = lax.all_to_all(row_sums, GY, 0, 0, tiled=True)

    image_index = lax.axis_index(GX) * row_count // PATCHES
    tenant = lax.dynamic_slice_in_dim(tenant_of_image, image_index, 1, 0)
    rotation = cayley(tenant, oft_skew)
    turned = rotate(tokens, row_sums, ln_gain[None], rotation, local_width * group)

    out_own = w_out.reshape(head_dim, w_out.shape[2])
    qkv_own = w_qkv.transpose(1, 2, 0, 3)[0]
    layers, lines = lax.axis_size("zl"), lax.axis_size("y")
    column = jnp.stack([turned] + [mirror(turned, "zl", mask) for mask in range(1, layers)])
    column, *own = lax.optimization_barrier((column, qkv_own, w_up, w_down, out_own))
    qkv_other, far_side = swap(own[0]), swap(jnp.concatenate(own[1:], 0))
    far_rows, near_rows = reorder(from_ahead(column, "y"), row_source, across)
    far_rows = far_rows.reshape(-1, local_width)
    near_rows = near_rows.reshape(-1, local_width)
    far_rows, qkv_other, far_side = lax.optimization_barrier((far_rows, qkv_other, far_side))
    second_other = far_side[local_width:]
    first = (qkv_own, qkv_other, w_up, far_side)
    second = jnp.concatenate([w_down, second_other[:-head_dim], out_own, second_other[-head_dim:]], 0)

    far_total, came = sum_along_x(far_rows, first, ())
    split = 2 * qkv_cols
    far_total = far_total.astype(jnp.bfloat16)
    far_qkv, far_up = shift(far_total[:, :split], "zh", 1), shift(far_total[:, split:], "zh", 1)
    total, _ = sum_along_x(near_rows, first, came)
    queries, pair = heads(total, far_qkv, q_gains, k_gains)
    attended = attention(queries, pair, swap(pair))
    up_pre = total[:, split:] + far_up.astype(jnp.float32) + bias
    hidden = jax.nn.gelu(up_pre, approximate=False).astype(jnp.bfloat16)

    value = jnp.concatenate([hidden, attended], 1)
    partner = shift(value, "zh", 1)
    given = [jnp.concatenate(share_along_x(value), 0), *share_along_x(partner)]
    parts = [
        matmul(rows, second).astype(jnp.bfloat16).reshape(-1, row_count, local_width) for rows in given
    ]
    outgoing = reorder(parts, owner_source, lines)
    sent = {k: shift(outgoing[k], "y", k) for k in FAR_FIRST}
    total = outgoing[0].astype(jnp.float32)
    for k in FAR_FIRST:
        total = total + sent[k].astype(jnp.float32)
    returned = lax.all_to_all(total.astype(jnp.bfloat16), "zl", 0, 0, tiled=True)
    mixed = jnp.sum(returned.astype(jnp.float32), 0)
    return (floats + mixed + down_bias).astype(jnp.bfloat16)


def solution(mesh):
    names = tuple(name for name, _ in AXES)
    sizes = tuple(size for _, size in AXES)
    fine_mesh = Mesh(mesh.devices.reshape(sizes), names)
    in_specs = (
        P(GX, GY),
        P(GY),
        P(None, GY, None, None),
        P(),
        P(GY, GX, None, None),
        P(GY, GX),
        P(GX),
        P(GX, None),
        P(GX, None),
        P(GX, None, GY),
        P(GX, GY),
        P(GY),
    )
    return jax.shard_map(
        per_device, mesh=fine_mesh, in_specs=in_specs, out_specs=P(GX, GY), check_vma=False
    )
```

```python
import functools

import jax
import jax.numpy as jnp
from jax import lax
from jax.experimental import pallas as pl
from jax.experimental.pallas import tpu as pltpu
from jax.sharding import Mesh
from jax.sharding import PartitionSpec as P

PATCHES = 256
HIGH = lax.Precision.HIGHEST
AXES = (("zl", 4), ("y", 4), ("core", 2), ("zh", 2), ("x", 4))
GX = ("zl", "y", "core")
GY = ("zh", "x")
FAR_FIRST = (2, 1, 3)


def split_bf16(value):
    high = value.astype(jnp.bfloat16)
    low = (value - high.astype(jnp.float32)).astype(jnp.bfloat16)
    return high, low

def dot3(left, right):
    left_high, left_low = left
    right_high, right_low = right
    return jnp.dot(
        jnp.concatenate([left_high, left_high, left_low], 1),
        jnp.concatenate([right_high, right_low, right_high], 0),
        preferred_element_type=jnp.float32,
    )

def cayley_kernel(tenant_ref, raw_ref, rotation_ref, skew_ref, inverse_ref):
    count, order = raw_ref.shape[1], raw_ref.shape[2]
    identity = (
        lax.broadcasted_iota(jnp.int32, (order, order), 0)
        == lax.broadcasted_iota(jnp.int32, (order, order), 1)
    ).astype(jnp.float32)
    bounds = []
    for block in range(count):
        raw = raw_ref[0, block]
        skew = 0.5 * (raw.T - raw)
        parts = split_bf16(skew)
        skew_ref[block] = skew
        gram = identity - dot3(parts, parts)
        bounds.append(1.001 * jnp.sqrt(0.5 * jnp.sum(gram * gram, keepdims=True)))
        inverse_ref[block] = gram
    top = functools.reduce(jnp.maximum, bounds)
    least = 1.0 / top
    scale = 2.0 * top / (1.0 + top)
    for block in range(count):
        start = (identity + skew_ref[block]) * least
        ratio = inverse_ref[block] * (least * scale)
        update = dot3(split_bf16(start), split_bf16(ratio))
        inverse_ref[block] = scale * (2.0 * start - update)
    least = 4.0 * top / ((1.0 + top) * (1.0 + top))

    def step(scale):
        for block in range(count):
            inverse = inverse_ref[block]
            parts = split_bf16(inverse)
            product = inverse - dot3(split_bf16(skew_ref[block]), parts)
            update = dot3(parts, split_bf16(product * scale))
            inverse_ref[block] = scale * (2.0 * inverse - update)

    def keep_going(carry):
        return carry[0, 0] < 0.9995

    def scaled_step(carry):
        step(2.0 / (1.0 + carry))
        return 4.0 * carry / ((1.0 + carry) * (1.0 + carry))

    lax.while_loop(keep_going, scaled_step, least)
    for block in range(count):
        inverse = inverse_ref[block]
        skew = skew_ref[block]
        rest = identity - inverse + jnp.dot(skew, inverse, precision=HIGH, preferred_element_type=jnp.float32)
        fixed = inverse + dot3(split_bf16(inverse), split_bf16(rest))
        rotation_ref[block] = 2.0 * fixed - identity

def cayley(tenant, oft_skew):
    count, order = oft_skew.shape[1], oft_skew.shape[2]
    return pl.pallas_call(
        cayley_kernel,
        out_shape=jax.ShapeDtypeStruct((count, order, order), jnp.float32),
        grid_spec=pltpu.PrefetchScalarGridSpec(
            num_scalar_prefetch=1,
            grid=(1,),
            in_specs=[pl.BlockSpec((1, count, order, order), lambda i, tenant: (tenant[0], 0, 0, 0))],
            out_specs=pl.BlockSpec((count, order, order), lambda i, tenant: (0, 0, 0)),
            scratch_shapes=[
                pltpu.VMEM((count, order, order), jnp.float32),
                pltpu.VMEM((count, order, order), jnp.float32),
            ],
        ),
        compiler_params=pltpu.CompilerParams(vmem_limit_bytes=60 << 20),
        cost_estimate=pl.CostEstimate(flops=20_000_000_000, bytes_accessed=2_000_000, transcendentals=0),
    )(tenant, oft_skew)


def rotate_kernel(full_width, tokens_ref, gain_ref, rotation_ref, sums_ref, turned_ref):
    rows, order = tokens_ref.shape[0], rotation_ref.shape[1]
    sums = jnp.broadcast_to(jnp.sum(sums_ref[...], 0), (rows, 2 * rows))
    lane = lax.broadcasted_iota(jnp.int32, sums.shape, 1)
    row = lax.broadcasted_iota(jnp.int32, sums.shape, 0)
    total = jnp.sum(jnp.where(lane == row, sums, 0.0), 1, keepdims=True)
    squares = jnp.sum(jnp.where(lane == row + rows, sums, 0.0), 1, keepdims=True)
    row_mean = total / full_width
    row_var = squares / full_width - row_mean * row_mean
    row_scale = lax.rsqrt(row_var + 1e-06)
    for block in range(rotation_ref.shape[0]):
        columns = pl.ds(block * order, order)
        floats = tokens_ref[:, columns].astype(jnp.float32)
        normed = (floats - row_mean) * row_scale * gain_ref[:, columns]
        turned = jnp.dot(
            normed, rotation_ref[block], precision=HIGH, preferred_element_type=jnp.float32
        )
        turned_ref[:, columns] = turned.astype(jnp.bfloat16)


def rotate(tokens, sums, gain, rotation, full_width):
    return pl.pallas_call(
        functools.partial(rotate_kernel, full_width),
        out_shape=jax.ShapeDtypeStruct(tokens.shape, jnp.bfloat16),
        cost_estimate=pl.CostEstimate(
            flops=600_000_000, bytes_accessed=1_000_000, transcendentals=0
        ),
    )(tokens, gain, rotation, sums)


def head_norm(values_in, gain):
    width_count = values_in.shape[-1]
    row_mean = jnp.sum(values_in, -1, keepdims=True) / width_count
    row_var = jnp.sum(values_in * values_in, -1, keepdims=True) / width_count - row_mean * row_mean
    return (values_in - row_mean) * lax.rsqrt(row_var + 1e-06) * gain


def heads_kernel(sum_ref, far_ref, q_gain_ref, k_gain_ref, queries_ref, pair_ref):
    head_dim = q_gain_ref.shape[-1]
    for head in range(2):
        columns = pl.ds(head * 3 * head_dim, 3 * head_dim)
        qkv = sum_ref[:, columns] + far_ref[:, columns].astype(jnp.float32)
        queries = head_norm(qkv[:, :head_dim], q_gain_ref[head])
        keys_normed = head_norm(qkv[:, head_dim : 2 * head_dim], k_gain_ref[head])
        queries_ref[head] = queries.astype(jnp.bfloat16)
        pair_ref[head, 0] = keys_normed.astype(jnp.bfloat16)
        pair_ref[head, 1] = qkv[:, 2 * head_dim :].astype(jnp.bfloat16)


def heads(total, far, q_gain, k_gain):
    rows, columns = far.shape
    head_dim = q_gain.shape[-1]
    return pl.pallas_call(
        heads_kernel,
        out_shape=(
            jax.ShapeDtypeStruct((2, rows, head_dim), jnp.bfloat16),
            jax.ShapeDtypeStruct((2, 2, rows, head_dim), jnp.bfloat16),
        ),
        grid=(1,),
        in_specs=[
            pl.BlockSpec((rows, columns), lambda i: (0, 0)),
            pl.BlockSpec((rows, columns), lambda i: (0, 0)),
            pl.BlockSpec((2, 1, head_dim), lambda i: (0, 0, 0)),
            pl.BlockSpec((2, 1, head_dim), lambda i: (0, 0, 0)),
        ],
        out_specs=(
            pl.BlockSpec((2, rows, head_dim), lambda i: (0, 0, 0)),
            pl.BlockSpec((2, 2, rows, head_dim), lambda i: (0, 0, 0, 0)),
        ),
        cost_estimate=pl.CostEstimate(
            flops=10_000_000, bytes_accessed=2_000_000, transcendentals=0
        ),
    )(total, far, q_gain, k_gain)


def attention_kernel(queries_ref, pair_ref, other_ref, attended_ref):
    head_dim = queries_ref.shape[-1]
    for head in range(2):
        keys = jnp.concatenate([pair_ref[head, 0], other_ref[1 - head, 0]], 0)
        values = jnp.concatenate([pair_ref[head, 1], other_ref[1 - head, 1]], 0)
        scores = lax.dot_general(
            queries_ref[head], keys, (((1,), (1,)), ((), ())), preferred_element_type=jnp.float32
        ) / jnp.sqrt(jnp.float32(head_dim))
        expo = jnp.exp(scores - jnp.max(scores, -1, keepdims=True))
        weights = (expo / jnp.sum(expo, -1, keepdims=True)).astype(jnp.bfloat16)
        attended = jnp.dot(weights, values, preferred_element_type=jnp.float32)
        attended_ref[:, head * head_dim : (head + 1) * head_dim] = attended.astype(jnp.bfloat16)


def attention(queries, pair, other):
    heads_here, rows, head_dim = queries.shape
    return pl.pallas_call(
        attention_kernel,
        out_shape=jax.ShapeDtypeStruct((rows, heads_here * head_dim), jnp.bfloat16),
        cost_estimate=pl.CostEstimate(
            flops=40_000_000, bytes_accessed=1_000_000, transcendentals=70_000
        ),
    )(queries, pair, other)


def reorder_kernel(source, given, *refs):
    blocks_refs, ordered_refs, held_ref = refs[:given], refs[given:-1], refs[-1]
    at = 0
    for blocks_ref in blocks_refs:
        held_ref[at : at + blocks_ref.shape[0]] = blocks_ref[...]
        at += blocks_ref.shape[0]
    place = 0
    for ordered_ref in ordered_refs:
        for row in range(ordered_ref.shape[0]):
            ordered_ref[row] = held_ref[source(place)]
            place += 1


def reorder(parts, source, sizes):
    count = sum(sizes)
    block = parts[0].shape[1:]
    return pl.pallas_call(
        functools.partial(reorder_kernel, source, len(parts)),
        out_shape=tuple(jax.ShapeDtypeStruct((size, *block), parts[0].dtype) for size in sizes),
        scratch_shapes=[pltpu.VMEM((count, *block), parts[0].dtype)],
        cost_estimate=pl.CostEstimate(flops=0, bytes_accessed=3_000_000, transcendentals=0),
    )(*parts)


def row_source(place):
    second = place % 2
    half, step = ((1 - place // 2, 2) if place < 4 else (1 - (place - 4) // 6, (0, 1, 3)[(place - 4) % 6 // 2]))
    x = lax.rem(lax.axis_index("x") + step, 4)
    image = (lax.axis_index("zh") ^ half) * 4 + x
    line = lax.rem(4 + image % 2 * 2 + second - lax.axis_index("y"), 4)
    return line * 4 + (image // 2 ^ lax.axis_index("zl"))


def owner_source(place):
    line = lax.rem(lax.axis_index("y") + place // 4, 4)
    image = place % 4 * 2 + line // 2
    step = lax.rem(4 + image % 4 - lax.axis_index("x"), 4)
    return (image // 4 ^ lax.axis_index("zh")) * 8 + (step ^ step // 2) * 2 + line % 2


def swap(value):
    return lax.ppermute(value, "core", [(0, 1), (1, 0)])


def shift(value, axis, distance):
    size = lax.axis_size(axis)
    return lax.ppermute(value, axis, [(i, (i + distance) % size) for i in range(size)])


def mirror(value, axis, mask):
    return lax.ppermute(value, axis, [(i, i ^ mask) for i in range(lax.axis_size(axis))])


def from_ahead(value, axis):
    size = lax.axis_size(axis)
    sent = {k: shift(value, axis, k) for k in FAR_FIRST}
    return [value] + [sent[size - k] for k in range(1, size)]


def products_kernel(rows_ref, own_ref, other_ref, up_ref, up_far_ref, *refs):
    piece_refs, weights = refs[:-1], refs[-1]
    step = pl.program_id(0)
    for first, qkv_ref in enumerate((own_ref, other_ref)):

        @pl.when(step == first)
        def _(qkv_ref=qkv_ref):
            weights[...] = jnp.concatenate([qkv_ref[part] for part in range(3)], 1)

    tiles = (pl.num_programs(0) - 2) // 2

    @pl.when(jnp.logical_and(step >= 2, step < 2 + tiles))
    def _():
        weights[...] = up_ref[...]

    @pl.when(step >= 2 + tiles)
    def _():
        weights[...] = up_far_ref[...]

    product = jnp.dot(rows_ref[...], weights[...], preferred_element_type=jnp.float32)
    at = 0
    for piece_ref in piece_refs:
        piece_ref[...] = product[at : at + piece_ref.shape[0]].astype(piece_ref.dtype)
        at += piece_ref.shape[0]


def products(rows, qkv_own, qkv_other, up_own, far_side, pieces):
    row_count, depth = rows.shape
    parts, _, head_dim = qkv_own.shape
    tile = parts * head_dim
    tiles = up_own.shape[1] // tile
    columns = (2 + 2 * tiles) * tile
    whole = pl.BlockSpec((parts, depth, head_dim), lambda i: (0, 0, 0))
    return pl.pallas_call(
        products_kernel,
        out_shape=tuple(jax.ShapeDtypeStruct((size, columns), dtype) for size, dtype in pieces),
        grid=(2 + 2 * tiles,),
        in_specs=[
            pl.BlockSpec((row_count, depth), lambda i: (0, 0)),
            whole,
            whole,
            pl.BlockSpec((depth, tile), lambda i: (0, jnp.clip(i - 2, 0, tiles - 1))),
            pl.BlockSpec((depth, tile), lambda i: (0, jnp.clip(i - 2 - tiles, 0, tiles - 1))),
        ],
        out_specs=tuple(pl.BlockSpec((size, tile), lambda i: (0, i)) for size, _ in pieces),
        scratch_shapes=[pltpu.VMEM((depth, tile), jnp.bfloat16)],
        cost_estimate=pl.CostEstimate(
            flops=2 * row_count * depth * columns, bytes_accessed=8_000_000, transcendentals=0
        ),
    )(rows, qkv_own, qkv_other, up_own, far_side)


def sum_along_x(two_steps, others, after):
    here, ahead_low, ahead_high, behind_low, behind_high = others
    low, high = lax.optimization_barrier((two_steps, after[:1]))[0]
    first = (shift(low, "x", 1), shift(high, "x", -1))
    ahead_low = (ahead_low + first[0].astype(jnp.float32)).astype(jnp.bfloat16)
    behind_high = (behind_high + first[1].astype(jnp.float32)).astype(jnp.bfloat16)
    ahead = jnp.concatenate([ahead_low, ahead_high], 0)
    behind = jnp.concatenate([behind_low, behind_high], 0)
    ahead, behind = lax.optimization_barrier(((ahead, behind), after[1:]))[0]
    sums = (ahead, behind)
    ahead, behind = shift(ahead, "x", 1), shift(behind, "x", -1)
    return here + ahead.astype(jnp.float32) + behind.astype(jnp.float32), (sums, (ahead, behind))


def share_along_x(value):
    half = value.shape[0] // 2
    behind, ahead = shift(value, "x", 1), shift(value, "x", -1)
    across = [shift(behind[:half], "x", 1), shift(ahead[half:], "x", -1)]
    return jnp.concatenate([value, ahead, behind], 0), jnp.concatenate(across, 0)


def matmul(left, right):
    return jnp.dot(left, right, preferred_element_type=jnp.float32)


def per_device(
    tokens,
    ln_gain,
    oft_skew,
    tenant_of_image,
    w_qkv,
    w_up,
    up_bias,
    q_gain,
    k_gain,
    w_out,
    w_down,
    down_bias,
):
    row_count, local_width = tokens.shape
    head_dim = w_qkv.shape[3]
    qkv_cols = 3 * head_dim
    across, along = lax.axis_size("zh"), lax.axis_size("x")
    group = across * along

    hidden_width = up_bias.shape[0]
    small_own = jnp.concatenate([up_bias[None], q_gain, k_gain], 1)
    small = jnp.stack([small_own, swap(small_own)])
    bias = small[:, 0, :hidden_width].reshape(2 * hidden_width)
    q_gains = small[:, :, hidden_width : hidden_width + head_dim]
    k_gains = small[:, :, hidden_width + head_dim :]

    floats = tokens.astype(jnp.float32)
    row_sums = jnp.concatenate([jnp.sum(floats, 1), jnp.sum(floats * floats, 1)])[None]
    row_sums = jnp.broadcast_to(row_sums[None], (group, 1, 2 * row_count))
    row_sums = lax.all_to_all(row_sums, GY, 0, 0, tiled=True)

    image_index = lax.axis_index(GX) * row_count // PATCHES
    tenant = lax.dynamic_slice_in_dim(tenant_of_image, image_index, 1, 0)
    rotation = cayley(tenant, oft_skew)
    turned = rotate(tokens, row_sums, ln_gain[None], rotation, local_width * group)

    out_own = w_out.reshape(head_dim, w_out.shape[2])
    qkv_own = w_qkv.transpose(1, 2, 0, 3)[0]
    layers, lines = lax.axis_size("zl"), lax.axis_size("y")
    column = jnp.stack([turned] + [mirror(turned, "zl", mask) for mask in range(1, layers)])
    column, *own = lax.optimization_barrier((column, qkv_own, w_up, w_down, out_own))
    qkv_other, far_side = swap(own[0]), swap(jnp.concatenate(own[1:], 0))
    two_steps, others = reorder(from_ahead(column, "y"), row_source, (4, 12))
    two_steps = two_steps.reshape(-1, local_width)
    others = others.reshape(-1, local_width)
    two_steps, qkv_other, far_side = lax.optimization_barrier((two_steps, qkv_other, far_side))
    second_other = far_side[local_width:]
    second = jnp.concatenate([w_down, second_other[:-head_dim], out_own, second_other[-head_dim:]], 0)
    first = (qkv_own, qkv_other, w_up, far_side)
    sent = (row_count, jnp.bfloat16)
    added = (row_count, jnp.float32)
    half_pieces = ((2 * row_count, jnp.float32), added, sent, sent, added)
    two_steps = products(two_steps, *first, (sent,) * 4)
    others, two_steps = lax.optimization_barrier((others, two_steps))
    others = products(others, *first, half_pieces * 2)
    far_total, came = sum_along_x(two_steps[:2], others[:5], ())
    split = 2 * qkv_cols
    far_total = far_total.astype(jnp.bfloat16)
    far_qkv, far_up = shift(far_total[:, :split], "zh", 1), shift(far_total[:, split:], "zh", 1)
    total, _ = sum_along_x(two_steps[2:], others[5:], came)
    queries, pair = heads(total, far_qkv, q_gains, k_gains)
    attended = attention(queries, pair, swap(pair))
    up_pre = total[:, split:] + far_up.astype(jnp.float32) + bias
    hidden = jax.nn.gelu(up_pre, approximate=False).astype(jnp.bfloat16)

    value = jnp.concatenate([hidden, attended], 1)
    partner = shift(value, "zh", 1)
    given = [jnp.concatenate(share_along_x(value), 0), *share_along_x(partner)]
    parts = [
        matmul(rows, second).astype(jnp.bfloat16).reshape(-1, row_count, local_width) for rows in given
    ]
    outgoing = reorder(parts, owner_source, (layers,) * lines)
    sent = {k: shift(outgoing[k], "y", k) for k in FAR_FIRST}
    total = outgoing[0].astype(jnp.float32)
    for k in FAR_FIRST:
        total = total + sent[k].astype(jnp.float32)
    returned = lax.all_to_all(total.astype(jnp.bfloat16), "zl", 0, 0, tiled=True)
    mixed = jnp.sum(returned.astype(jnp.float32), 0)
    return (floats + mixed + down_bias).astype(jnp.bfloat16)


def solution(mesh):
    names = tuple(name for name, _ in AXES)
    sizes = tuple(size for _, size in AXES)
    fine_mesh = Mesh(mesh.devices.reshape(sizes), names)
    in_specs = (
        P(GX, GY),
        P(GY),
        P(None, GY, None, None),
        P(),
        P(GY, GX, None, None),
        P(GY, GX),
        P(GX),
        P(GX, None),
        P(GX, None),
        P(GX, None, GY),
        P(GX, GY),
        P(GY),
    )
    return jax.shard_map(
        per_device, mesh=fine_mesh, in_specs=in_specs, out_specs=P(GX, GY), check_vma=False
    )
```

```python
import functools

import jax
import jax.numpy as jnp
from jax import lax
from jax.experimental import pallas as pl
from jax.experimental.pallas import tpu as pltpu
from jax.sharding import Mesh
from jax.sharding import PartitionSpec as P

PATCHES = 256
HIGH = lax.Precision.HIGHEST
AXES = (("zl", 4), ("y", 4), ("core", 2), ("zh", 2), ("x", 4))
GX = ("zl", "y", "core")
GY = ("zh", "x")
FAR_FIRST = (2, 1, 3)


def split_bf16(value):
    high = value.astype(jnp.bfloat16)
    low = (value - high.astype(jnp.float32)).astype(jnp.bfloat16)
    return high, low

def dot3(left, right):
    left_high, left_low = left
    right_high, right_low = right
    return jnp.dot(
        jnp.concatenate([left_high, left_high, left_low], 1),
        jnp.concatenate([right_high, right_low, right_high], 0),
        preferred_element_type=jnp.float32,
    )

def cayley_kernel(tenant_ref, raw_ref, rotation_ref, skew_ref, inverse_ref):
    count, order = raw_ref.shape[1], raw_ref.shape[2]
    identity = (
        lax.broadcasted_iota(jnp.int32, (order, order), 0)
        == lax.broadcasted_iota(jnp.int32, (order, order), 1)
    ).astype(jnp.float32)
    bounds = []
    for block in range(count):
        raw = raw_ref[0, block]
        skew = 0.5 * (raw.T - raw)
        parts = split_bf16(skew)
        skew_ref[block] = skew
        gram = identity - dot3(parts, parts)
        bounds.append(1.001 * jnp.sqrt(0.5 * jnp.sum(gram * gram, keepdims=True)))
        inverse_ref[block] = gram
    top = functools.reduce(jnp.maximum, bounds)
    least = 1.0 / top
    scale = 2.0 * top / (1.0 + top)
    for block in range(count):
        start = (identity + skew_ref[block]) * least
        ratio = inverse_ref[block] * (least * scale)
        update = dot3(split_bf16(start), split_bf16(ratio))
        inverse_ref[block] = scale * (2.0 * start - update)
    least = 4.0 * top / ((1.0 + top) * (1.0 + top))

    def step(scale):
        for block in range(count):
            inverse = inverse_ref[block]
            parts = split_bf16(inverse)
            product = inverse - dot3(split_bf16(skew_ref[block]), parts)
            update = dot3(parts, split_bf16(product * scale))
            inverse_ref[block] = scale * (2.0 * inverse - update)

    def keep_going(carry):
        return carry[0, 0] < 0.9995

    def scaled_step(carry):
        step(2.0 / (1.0 + carry))
        return 4.0 * carry / ((1.0 + carry) * (1.0 + carry))

    lax.while_loop(keep_going, scaled_step, least)
    for block in range(count):
        inverse = inverse_ref[block]
        skew = skew_ref[block]
        rest = identity - inverse + jnp.dot(skew, inverse, precision=HIGH, preferred_element_type=jnp.float32)
        fixed = inverse + dot3(split_bf16(inverse), split_bf16(rest))
        rotation_ref[block] = 2.0 * fixed - identity

def cayley(tenant, oft_skew):
    count, order = oft_skew.shape[1], oft_skew.shape[2]
    return pl.pallas_call(
        cayley_kernel,
        out_shape=jax.ShapeDtypeStruct((count, order, order), jnp.float32),
        grid_spec=pltpu.PrefetchScalarGridSpec(
            num_scalar_prefetch=1,
            grid=(1,),
            in_specs=[pl.BlockSpec((1, count, order, order), lambda i, tenant: (tenant[0], 0, 0, 0))],
            out_specs=pl.BlockSpec((count, order, order), lambda i, tenant: (0, 0, 0)),
            scratch_shapes=[
                pltpu.VMEM((count, order, order), jnp.float32),
                pltpu.VMEM((count, order, order), jnp.float32),
            ],
        ),
        compiler_params=pltpu.CompilerParams(vmem_limit_bytes=60 << 20),
        cost_estimate=pl.CostEstimate(flops=20_000_000_000, bytes_accessed=2_000_000, transcendentals=0),
    )(tenant, oft_skew)


def rotate_kernel(full_width, tokens_ref, gain_ref, rotation_ref, sums_ref, turned_ref):
    rows, order = tokens_ref.shape[0], rotation_ref.shape[1]
    sums = jnp.broadcast_to(jnp.sum(sums_ref[...], 0), (rows, 2 * rows))
    lane = lax.broadcasted_iota(jnp.int32, sums.shape, 1)
    row = lax.broadcasted_iota(jnp.int32, sums.shape, 0)
    total = jnp.sum(jnp.where(lane == row, sums, 0.0), 1, keepdims=True)
    squares = jnp.sum(jnp.where(lane == row + rows, sums, 0.0), 1, keepdims=True)
    row_mean = total / full_width
    row_var = squares / full_width - row_mean * row_mean
    row_scale = lax.rsqrt(row_var + 1e-06)
    for block in range(rotation_ref.shape[0]):
        columns = pl.ds(block * order, order)
        floats = tokens_ref[:, columns].astype(jnp.float32)
        normed = (floats - row_mean) * row_scale * gain_ref[:, columns]
        turned = jnp.dot(
            normed, rotation_ref[block], precision=HIGH, preferred_element_type=jnp.float32
        )
        turned_ref[:, columns] = turned.astype(jnp.bfloat16)


def rotate(tokens, sums, gain, rotation, full_width):
    return pl.pallas_call(
        functools.partial(rotate_kernel, full_width),
        out_shape=jax.ShapeDtypeStruct(tokens.shape, jnp.bfloat16),
        cost_estimate=pl.CostEstimate(
            flops=600_000_000, bytes_accessed=1_000_000, transcendentals=0
        ),
    )(tokens, gain, rotation, sums)


def head_norm(values_in, gain):
    width_count = values_in.shape[-1]
    row_mean = jnp.sum(values_in, -1, keepdims=True) / width_count
    row_var = jnp.sum(values_in * values_in, -1, keepdims=True) / width_count - row_mean * row_mean
    return (values_in - row_mean) * lax.rsqrt(row_var + 1e-06) * gain


def heads_kernel(sum_ref, far_ref, q_gain_ref, k_gain_ref, queries_ref, pair_ref):
    head_dim = q_gain_ref.shape[-1]
    for head in range(2):
        columns = pl.ds(head * 3 * head_dim, 3 * head_dim)
        qkv = sum_ref[:, columns] + far_ref[:, columns].astype(jnp.float32)
        queries = head_norm(qkv[:, :head_dim], q_gain_ref[head])
        keys_normed = head_norm(qkv[:, head_dim : 2 * head_dim], k_gain_ref[head])
        queries_ref[head] = queries.astype(jnp.bfloat16)
        pair_ref[head, 0] = keys_normed.astype(jnp.bfloat16)
        pair_ref[head, 1] = qkv[:, 2 * head_dim :].astype(jnp.bfloat16)


def heads(total, far, q_gain, k_gain):
    rows, columns = far.shape
    head_dim = q_gain.shape[-1]
    return pl.pallas_call(
        heads_kernel,
        out_shape=(
            jax.ShapeDtypeStruct((2, rows, head_dim), jnp.bfloat16),
            jax.ShapeDtypeStruct((2, 2, rows, head_dim), jnp.bfloat16),
        ),
        grid=(1,),
        in_specs=[
            pl.BlockSpec((rows, columns), lambda i: (0, 0)),
            pl.BlockSpec((rows, columns), lambda i: (0, 0)),
            pl.BlockSpec((2, 1, head_dim), lambda i: (0, 0, 0)),
            pl.BlockSpec((2, 1, head_dim), lambda i: (0, 0, 0)),
        ],
        out_specs=(
            pl.BlockSpec((2, rows, head_dim), lambda i: (0, 0, 0)),
            pl.BlockSpec((2, 2, rows, head_dim), lambda i: (0, 0, 0, 0)),
        ),
        cost_estimate=pl.CostEstimate(
            flops=10_000_000, bytes_accessed=2_000_000, transcendentals=0
        ),
    )(total, far, q_gain, k_gain)


def attention_kernel(queries_ref, pair_ref, other_ref, attended_ref):
    head_dim = queries_ref.shape[-1]
    for head in range(2):
        keys = jnp.concatenate([pair_ref[head, 0], other_ref[1 - head, 0]], 0)
        values = jnp.concatenate([pair_ref[head, 1], other_ref[1 - head, 1]], 0)
        scores = lax.dot_general(
            queries_ref[head], keys, (((1,), (1,)), ((), ())), preferred_element_type=jnp.float32
        ) / jnp.sqrt(jnp.float32(head_dim))
        expo = jnp.exp(scores - jnp.max(scores, -1, keepdims=True))
        weights = (expo / jnp.sum(expo, -1, keepdims=True)).astype(jnp.bfloat16)
        attended = jnp.dot(weights, values, preferred_element_type=jnp.float32)
        attended_ref[:, head * head_dim : (head + 1) * head_dim] = attended.astype(jnp.bfloat16)


def attention(queries, pair, other):
    heads_here, rows, head_dim = queries.shape
    return pl.pallas_call(
        attention_kernel,
        out_shape=jax.ShapeDtypeStruct((rows, heads_here * head_dim), jnp.bfloat16),
        cost_estimate=pl.CostEstimate(
            flops=40_000_000, bytes_accessed=1_000_000, transcendentals=70_000
        ),
    )(queries, pair, other)


def reorder_kernel(source, given, *refs):
    blocks_refs, ordered_refs, held_ref = refs[:given], refs[given:-1], refs[-1]
    at = 0
    for blocks_ref in blocks_refs:
        held_ref[at : at + blocks_ref.shape[0]] = blocks_ref[...]
        at += blocks_ref.shape[0]
    place = 0
    for ordered_ref in ordered_refs:
        for row in range(ordered_ref.shape[0]):
            ordered_ref[row] = held_ref[source(place)]
            place += 1


def reorder(parts, source, sizes):
    count = sum(sizes)
    block = parts[0].shape[1:]
    return pl.pallas_call(
        functools.partial(reorder_kernel, source, len(parts)),
        out_shape=tuple(jax.ShapeDtypeStruct((size, *block), parts[0].dtype) for size in sizes),
        scratch_shapes=[pltpu.VMEM((count, *block), parts[0].dtype)],
        cost_estimate=pl.CostEstimate(flops=0, bytes_accessed=3_000_000, transcendentals=0),
    )(*parts)


def row_source(place):
    second = place % 2
    half, step = ((1 - place // 2, 2) if place < 4 else (1 - (place - 4) // 6, (0, 1, 3)[(place - 4) % 6 // 2]))
    x = lax.rem(lax.axis_index("x") + step, 4)
    image = (lax.axis_index("zh") ^ half) * 4 + x
    line = lax.rem(4 + image % 2 * 2 + second - lax.axis_index("y"), 4)
    return line * 4 + (image // 2 ^ lax.axis_index("zl"))


def owner_source(place):
    line = lax.rem(lax.axis_index("y") + place // 4, 4)
    image = place % 4 * 2 + line // 2
    step = lax.rem(4 + image % 4 - lax.axis_index("x"), 4)
    return (image // 4 ^ lax.axis_index("zh")) * 8 + (step ^ step // 2) * 2 + line % 2


def swap(value):
    return lax.ppermute(value, "core", [(0, 1), (1, 0)])


def shift(value, axis, distance):
    size = lax.axis_size(axis)
    return lax.ppermute(value, axis, [(i, (i + distance) % size) for i in range(size)])


def mirror(value, axis, mask):
    return lax.ppermute(value, axis, [(i, i ^ mask) for i in range(lax.axis_size(axis))])


def from_ahead(value, axis):
    size = lax.axis_size(axis)
    sent = {k: shift(value, axis, k) for k in FAR_FIRST}
    return [value] + [sent[size - k] for k in range(1, size)]


def products_kernel(rows_ref, own_ref, other_ref, up_ref, up_far_ref, *refs):
    piece_refs, weights = refs[:-1], refs[-1]
    step = pl.program_id(0)

    @pl.when(step == 0)
    def _():
        parts = [qkv_ref[part] for qkv_ref in (own_ref, other_ref) for part in range(3)]
        weights[...] = jnp.concatenate(parts, 1)

    @pl.when(step == 1)
    def _():
        weights[...] = up_ref[...]

    @pl.when(step == 2)
    def _():
        weights[...] = up_far_ref[...]

    product = jnp.dot(rows_ref[...], weights[...], preferred_element_type=jnp.float32)
    at = 0
    for piece_ref in piece_refs:
        piece_ref[...] = product[at : at + piece_ref.shape[0]].astype(piece_ref.dtype)
        at += piece_ref.shape[0]


def products(rows, qkv_own, qkv_other, up_own, far_side, pieces):
    row_count, depth = rows.shape
    parts, _, head_dim = qkv_own.shape
    tile = 2 * parts * head_dim
    assert up_own.shape[1] == tile
    columns = 3 * tile
    whole = pl.BlockSpec((parts, depth, head_dim), lambda i: (0, 0, 0))
    return pl.pallas_call(
        products_kernel,
        out_shape=tuple(jax.ShapeDtypeStruct((size, columns), dtype) for size, dtype in pieces),
        grid=(3,),
        in_specs=[
            pl.BlockSpec((row_count, depth), lambda i: (0, 0)),
            whole,
            whole,
            pl.BlockSpec((depth, tile), lambda i: (0, 0)),
            pl.BlockSpec((depth, tile), lambda i: (0, 0)),
        ],
        out_specs=tuple(pl.BlockSpec((size, tile), lambda i: (0, i)) for size, _ in pieces),
        scratch_shapes=[pltpu.VMEM((depth, tile), jnp.bfloat16)],
        compiler_params=pltpu.CompilerParams(vmem_limit_bytes=28 << 20),
        cost_estimate=pl.CostEstimate(
            flops=2 * row_count * depth * columns, bytes_accessed=8_000_000, transcendentals=0
        ),
    )(rows, qkv_own, qkv_other, up_own, far_side)


def sum_along_x(two_steps, others, after):
    here, ahead_low, ahead_high, behind_low, behind_high = others
    low, high = lax.optimization_barrier((two_steps, after[:1]))[0]
    first = (shift(low, "x", 1), shift(high, "x", -1))
    ahead_low = (ahead_low + first[0].astype(jnp.float32)).astype(jnp.bfloat16)
    behind_high = (behind_high + first[1].astype(jnp.float32)).astype(jnp.bfloat16)
    ahead = jnp.concatenate([ahead_low, ahead_high], 0)
    behind = jnp.concatenate([behind_low, behind_high], 0)
    ahead, behind = lax.optimization_barrier(((ahead, behind), after[1:]))[0]
    sums = (ahead, behind)
    ahead, behind = shift(ahead, "x", 1), shift(behind, "x", -1)
    return here + ahead.astype(jnp.float32) + behind.astype(jnp.float32), (sums, (ahead, behind))


def share_along_x(value):
    half = value.shape[0] // 2
    behind, ahead = shift(value, "x", 1), shift(value, "x", -1)
    across = [shift(behind[:half], "x", 1), shift(ahead[half:], "x", -1)]
    return jnp.concatenate([value, ahead, behind], 0), jnp.concatenate(across, 0)


def matmul(left, right):
    return jnp.dot(left, right, preferred_element_type=jnp.float32)


def per_device(
    tokens,
    ln_gain,
    oft_skew,
    tenant_of_image,
    w_qkv,
    w_up,
    up_bias,
    q_gain,
    k_gain,
    w_out,
    w_down,
    down_bias,
):
    row_count, local_width = tokens.shape
    head_dim = w_qkv.shape[3]
    qkv_cols = 3 * head_dim
    across, along = lax.axis_size("zh"), lax.axis_size("x")
    group = across * along

    hidden_width = up_bias.shape[0]
    small_own = jnp.concatenate([up_bias[None], q_gain, k_gain], 1)
    small = jnp.stack([small_own, swap(small_own)])
    bias = small[:, 0, :hidden_width].reshape(2 * hidden_width)
    q_gains = small[:, :, hidden_width : hidden_width + head_dim]
    k_gains = small[:, :, hidden_width + head_dim :]

    floats = tokens.astype(jnp.float32)
    row_sums = jnp.concatenate([jnp.sum(floats, 1), jnp.sum(floats * floats, 1)])[None]
    row_sums = jnp.broadcast_to(row_sums[None], (group, 1, 2 * row_count))
    row_sums = lax.all_to_all(row_sums, GY, 0, 0, tiled=True)

    image_index = lax.axis_index(GX) * row_count // PATCHES
    tenant = lax.dynamic_slice_in_dim(tenant_of_image, image_index, 1, 0)
    rotation = cayley(tenant, oft_skew)
    turned = rotate(tokens, row_sums, ln_gain[None], rotation, local_width * group)

    out_own = w_out.reshape(head_dim, w_out.shape[2])
    qkv_own = w_qkv.transpose(1, 2, 0, 3)[0]
    layers, lines = lax.axis_size("zl"), lax.axis_size("y")
    column = jnp.stack([turned] + [mirror(turned, "zl", mask) for mask in range(1, layers)])
    column, *own = lax.optimization_barrier((column, qkv_own, w_up, w_down, out_own))
    qkv_other, far_side = swap(own[0]), swap(jnp.concatenate(own[1:], 0))
    two_steps, others = reorder(from_ahead(column, "y"), row_source, (4, 12))
    two_steps = two_steps.reshape(-1, local_width)
    others = others.reshape(-1, local_width)
    two_steps, qkv_other, far_side = lax.optimization_barrier((two_steps, qkv_other, far_side))
    second_other = far_side[local_width:]
    second = jnp.concatenate([w_down, second_other[:-head_dim], out_own, second_other[-head_dim:]], 0)
    first = (qkv_own, qkv_other, w_up, far_side)
    sent = (row_count, jnp.bfloat16)
    added = (row_count, jnp.float32)
    half_pieces = ((2 * row_count, jnp.float32), added, sent, sent, added)
    two_steps = products(two_steps, *first, (sent,) * 4)
    others, two_steps = lax.optimization_barrier((others, two_steps))
    others = products(others, *first, half_pieces * 2)
    far_total, came = sum_along_x(two_steps[:2], others[:5], ())
    split = 2 * qkv_cols
    far_total = far_total.astype(jnp.bfloat16)
    far_qkv, far_up = shift(far_total[:, :split], "zh", 1), shift(far_total[:, split:], "zh", 1)
    total, _ = sum_along_x(two_steps[2:], others[5:], came)
    queries, pair = heads(total, far_qkv, q_gains, k_gains)
    attended = attention(queries, pair, swap(pair))
    far_up, pair = lax.optimization_barrier((far_up, pair))
    up_pre = total[:, split:] + far_up.astype(jnp.float32) + bias
    hidden = jax.nn.gelu(up_pre, approximate=False).astype(jnp.bfloat16)

    value = jnp.concatenate([hidden, attended], 1)
    partner = shift(value, "zh", 1)
    given = [jnp.concatenate(share_along_x(value), 0), *share_along_x(partner)]
    parts = [
        matmul(rows, second).astype(jnp.bfloat16).reshape(-1, row_count, local_width) for rows in given
    ]
    outgoing = reorder(parts, owner_source, (layers,) * lines)
    sent = {k: shift(outgoing[k], "y", k) for k in FAR_FIRST}
    total = outgoing[0].astype(jnp.float32)
    for k in FAR_FIRST:
        total = total + sent[k].astype(jnp.float32)
    returned = lax.all_to_all(total.astype(jnp.bfloat16), "zl", 0, 0, tiled=True)
    mixed = jnp.sum(returned.astype(jnp.float32), 0)
    return (floats + mixed + down_bias).astype(jnp.bfloat16)


def solution(mesh):
    names = tuple(name for name, _ in AXES)
    sizes = tuple(size for _, size in AXES)
    fine_mesh = Mesh(mesh.devices.reshape(sizes), names)
    in_specs = (
        P(GX, GY),
        P(GY),
        P(None, GY, None, None),
        P(),
        P(GY, GX, None, None),
        P(GY, GX),
        P(GX),
        P(GX, None),
        P(GX, None),
        P(GX, None, GY),
        P(GX, GY),
        P(GY),
    )
    return jax.shard_map(
        per_device, mesh=fine_mesh, in_specs=in_specs, out_specs=P(GX, GY), check_vma=False
    )
```

```python
import functools

import jax
import jax.numpy as jnp
from jax import lax
from jax.experimental import pallas as pl
from jax.experimental.pallas import tpu as pltpu
from jax.sharding import Mesh
from jax.sharding import PartitionSpec as P

PATCHES = 256
HIGH = lax.Precision.HIGHEST
AXES = (("zl", 4), ("y", 4), ("core", 2), ("zh", 2), ("x", 4))
GX = ("zl", "y", "core")
GY = ("zh", "x")
FAR_FIRST = (2, 1, 3)


def split_bf16(value):
    high = value.astype(jnp.bfloat16)
    low = (value - high.astype(jnp.float32)).astype(jnp.bfloat16)
    return high, low

def dot3(left, right):
    left_high, left_low = left
    right_high, right_low = right
    return jnp.dot(
        jnp.concatenate([left_high, left_high, left_low], 1),
        jnp.concatenate([right_high, right_low, right_high], 0),
        preferred_element_type=jnp.float32,
    )

def cayley_kernel(tenant_ref, raw_ref, rotation_ref, skew_ref, inverse_ref):
    count, order = raw_ref.shape[1], raw_ref.shape[2]
    identity = (
        lax.broadcasted_iota(jnp.int32, (order, order), 0)
        == lax.broadcasted_iota(jnp.int32, (order, order), 1)
    ).astype(jnp.float32)
    bounds = []
    for block in range(count):
        raw = raw_ref[0, block]
        skew = 0.5 * (raw.T - raw)
        parts = split_bf16(skew)
        skew_ref[block] = skew
        gram = identity - dot3(parts, parts)
        bounds.append(1.001 * jnp.sqrt(0.5 * jnp.sum(gram * gram, keepdims=True)))
        inverse_ref[block] = gram
    top = functools.reduce(jnp.maximum, bounds)
    least = 1.0 / top
    scale = 2.0 * top / (1.0 + top)
    for block in range(count):
        start = (identity + skew_ref[block]) * least
        ratio = inverse_ref[block] * (least * scale)
        update = dot3(split_bf16(start), split_bf16(ratio))
        inverse_ref[block] = scale * (2.0 * start - update)
    least = 4.0 * top / ((1.0 + top) * (1.0 + top))

    def step(scale):
        for block in range(count):
            inverse = inverse_ref[block]
            parts = split_bf16(inverse)
            product = inverse - dot3(split_bf16(skew_ref[block]), parts)
            update = dot3(parts, split_bf16(product * scale))
            inverse_ref[block] = scale * (2.0 * inverse - update)

    def keep_going(carry):
        return carry[0, 0] < 0.9995

    def scaled_step(carry):
        step(2.0 / (1.0 + carry))
        return 4.0 * carry / ((1.0 + carry) * (1.0 + carry))

    lax.while_loop(keep_going, scaled_step, least)
    for block in range(count):
        inverse = inverse_ref[block]
        skew = skew_ref[block]
        rest = identity - inverse + jnp.dot(skew, inverse, precision=HIGH, preferred_element_type=jnp.float32)
        fixed = inverse + dot3(split_bf16(inverse), split_bf16(rest))
        rotation_ref[block] = 2.0 * fixed - identity

def image_here():
    return lax.axis_index("zl") * 2 + lax.axis_index("y") // 2


def cayley(tenants, oft_skew):
    count, order = oft_skew.shape[1], oft_skew.shape[2]
    return pl.pallas_call(
        cayley_kernel,
        out_shape=jax.ShapeDtypeStruct((count, order, order), jnp.float32),
        grid_spec=pltpu.PrefetchScalarGridSpec(
            num_scalar_prefetch=1,
            grid=(1,),
            in_specs=[pl.BlockSpec((1, count, order, order), lambda i, tenants: (tenants[image_here()], 0, 0, 0))],
            out_specs=pl.BlockSpec((count, order, order), lambda i, tenants: (0, 0, 0)),
            scratch_shapes=[
                pltpu.VMEM((count, order, order), jnp.float32),
                pltpu.VMEM((count, order, order), jnp.float32),
            ],
        ),
        compiler_params=pltpu.CompilerParams(vmem_limit_bytes=60 << 20),
        cost_estimate=pl.CostEstimate(flops=20_000_000_000, bytes_accessed=2_000_000, transcendentals=0),
    )(tenants, oft_skew)


def rotate_kernel(full_width, tokens_ref, gain_ref, rotation_ref, sums_ref, turned_ref):
    rows, order = tokens_ref.shape[0], rotation_ref.shape[1]
    sums = jnp.broadcast_to(jnp.sum(sums_ref[...], 0), (rows, 2 * rows))
    lane = lax.broadcasted_iota(jnp.int32, sums.shape, 1)
    row = lax.broadcasted_iota(jnp.int32, sums.shape, 0)
    total = jnp.sum(jnp.where(lane == row, sums, 0.0), 1, keepdims=True)
    squares = jnp.sum(jnp.where(lane == row + rows, sums, 0.0), 1, keepdims=True)
    row_mean = total / full_width
    row_var = squares / full_width - row_mean * row_mean
    row_scale = lax.rsqrt(row_var + 1e-06)
    for block in range(rotation_ref.shape[0]):
        columns = pl.ds(block * order, order)
        floats = tokens_ref[:, columns].astype(jnp.float32)
        normed = (floats - row_mean) * row_scale * gain_ref[:, columns]
        turned = jnp.dot(
            normed, rotation_ref[block], precision=HIGH, preferred_element_type=jnp.float32
        )
        turned_ref[:, columns] = turned.astype(jnp.bfloat16)


def rotate(tokens, sums, gain, rotation, full_width):
    return pl.pallas_call(
        functools.partial(rotate_kernel, full_width),
        out_shape=jax.ShapeDtypeStruct(tokens.shape, jnp.bfloat16),
        cost_estimate=pl.CostEstimate(
            flops=600_000_000, bytes_accessed=1_000_000, transcendentals=0
        ),
    )(tokens, gain, rotation, sums)


def head_norm(values_in, gain):
    width_count = values_in.shape[-1]
    row_mean = jnp.sum(values_in, -1, keepdims=True) / width_count
    row_var = jnp.sum(values_in * values_in, -1, keepdims=True) / width_count - row_mean * row_mean
    return (values_in - row_mean) * lax.rsqrt(row_var + 1e-06) * gain


def heads_kernel(sum_ref, far_ref, q_gain_ref, k_gain_ref, queries_ref, pair_ref):
    head_dim = q_gain_ref.shape[-1]
    for head in range(2):
        columns = pl.ds(head * 3 * head_dim, 3 * head_dim)
        qkv = sum_ref[:, columns] + far_ref[:, columns].astype(jnp.float32)
        queries = head_norm(qkv[:, :head_dim], q_gain_ref[head])
        keys_normed = head_norm(qkv[:, head_dim : 2 * head_dim], k_gain_ref[head])
        queries_ref[head] = queries.astype(jnp.bfloat16)
        pair_ref[head, 0] = keys_normed.astype(jnp.bfloat16)
        pair_ref[head, 1] = qkv[:, 2 * head_dim :].astype(jnp.bfloat16)


def heads(total, far, q_gain, k_gain):
    rows, columns = far.shape
    head_dim = q_gain.shape[-1]
    return pl.pallas_call(
        heads_kernel,
        out_shape=(
            jax.ShapeDtypeStruct((2, rows, head_dim), jnp.bfloat16),
            jax.ShapeDtypeStruct((2, 2, rows, head_dim), jnp.bfloat16),
        ),
        grid=(1,),
        in_specs=[
            pl.BlockSpec((rows, columns), lambda i: (0, 0)),
            pl.BlockSpec((rows, columns), lambda i: (0, 0)),
            pl.BlockSpec((2, 1, head_dim), lambda i: (0, 0, 0)),
            pl.BlockSpec((2, 1, head_dim), lambda i: (0, 0, 0)),
        ],
        out_specs=(
            pl.BlockSpec((2, rows, head_dim), lambda i: (0, 0, 0)),
            pl.BlockSpec((2, 2, rows, head_dim), lambda i: (0, 0, 0, 0)),
        ),
        cost_estimate=pl.CostEstimate(
            flops=10_000_000, bytes_accessed=2_000_000, transcendentals=0
        ),
    )(total, far, q_gain, k_gain)


def attention_kernel(queries_ref, pair_ref, other_ref, attended_ref):
    head_dim = queries_ref.shape[-1]
    for head in range(2):
        keys = jnp.concatenate([pair_ref[head, 0], other_ref[1 - head, 0]], 0)
        values = jnp.concatenate([pair_ref[head, 1], other_ref[1 - head, 1]], 0)
        scores = lax.dot_general(
            queries_ref[head], keys, (((1,), (1,)), ((), ())), preferred_element_type=jnp.float32
        ) / jnp.sqrt(jnp.float32(head_dim))
        expo = jnp.exp(scores - jnp.max(scores, -1, keepdims=True))
        weights = (expo / jnp.sum(expo, -1, keepdims=True)).astype(jnp.bfloat16)
        attended = jnp.dot(weights, values, preferred_element_type=jnp.float32)
        attended_ref[:, head * head_dim : (head + 1) * head_dim] = attended.astype(jnp.bfloat16)


def attention(queries, pair, other):
    heads_here, rows, head_dim = queries.shape
    return pl.pallas_call(
        attention_kernel,
        out_shape=jax.ShapeDtypeStruct((rows, heads_here * head_dim), jnp.bfloat16),
        cost_estimate=pl.CostEstimate(
            flops=40_000_000, bytes_accessed=1_000_000, transcendentals=70_000
        ),
    )(queries, pair, other)


def reorder_kernel(source, given, *refs):
    blocks_refs, ordered_refs, held_ref = refs[:given], refs[given:-1], refs[-1]
    at = 0
    for blocks_ref in blocks_refs:
        held_ref[at : at + blocks_ref.shape[0]] = blocks_ref[...]
        at += blocks_ref.shape[0]
    place = 0
    for ordered_ref in ordered_refs:
        for row in range(ordered_ref.shape[0]):
            ordered_ref[row] = held_ref[source(place)]
            place += 1


def reorder(parts, source, sizes):
    count = sum(sizes)
    block = parts[0].shape[1:]
    return pl.pallas_call(
        functools.partial(reorder_kernel, source, len(parts)),
        out_shape=tuple(jax.ShapeDtypeStruct((size, *block), parts[0].dtype) for size in sizes),
        scratch_shapes=[pltpu.VMEM((count, *block), parts[0].dtype)],
        cost_estimate=pl.CostEstimate(flops=0, bytes_accessed=3_000_000, transcendentals=0),
    )(*parts)


def row_source(place):
    second = place % 2
    half, step = ((1 - place // 2, 2) if place < 4 else (1 - (place - 4) // 6, (0, 1, 3)[(place - 4) % 6 // 2]))
    x = lax.rem(lax.axis_index("x") + step, 4)
    image = (lax.axis_index("zh") ^ half) * 4 + x
    line = lax.rem(4 + image % 2 * 2 + second - lax.axis_index("y"), 4)
    return line * 4 + (image // 2 ^ lax.axis_index("zl"))


def owner_source(place):
    line = lax.rem(lax.axis_index("y") + place // 4, 4)
    image = place % 4 * 2 + line // 2
    step = lax.rem(4 + image % 4 - lax.axis_index("x"), 4)
    return (image // 4 ^ lax.axis_index("zh")) * 8 + (step ^ step // 2) * 2 + line % 2


def swap(value):
    return lax.ppermute(value, "core", [(0, 1), (1, 0)])


def shift(value, axis, distance):
    size = lax.axis_size(axis)
    return lax.ppermute(value, axis, [(i, (i + distance) % size) for i in range(size)])


def mirror(value, axis, mask):
    return lax.ppermute(value, axis, [(i, i ^ mask) for i in range(lax.axis_size(axis))])


def from_ahead(value, axis):
    size = lax.axis_size(axis)
    sent = {k: shift(value, axis, k) for k in FAR_FIRST}
    return [value] + [sent[size - k] for k in range(1, size)]


def products_kernel(rows_ref, own_ref, other_ref, up_ref, up_far_ref, *refs):
    piece_refs, weights = refs[:-1], refs[-1]
    step = pl.program_id(0)

    @pl.when(step == 0)
    def _():
        parts = [qkv_ref[part] for qkv_ref in (own_ref, other_ref) for part in range(3)]
        weights[...] = jnp.concatenate(parts, 1)

    @pl.when(step == 1)
    def _():
        weights[...] = up_ref[...]

    @pl.when(step == 2)
    def _():
        weights[...] = up_far_ref[...]

    product = jnp.dot(rows_ref[...], weights[...], preferred_element_type=jnp.float32)
    at = 0
    for piece_ref in piece_refs:
        piece_ref[...] = product[at : at + piece_ref.shape[0]].astype(piece_ref.dtype)
        at += piece_ref.shape[0]


def products(rows, qkv_own, qkv_other, up_own, far_side, pieces):
    row_count, depth = rows.shape
    parts, _, head_dim = qkv_own.shape
    tile = 2 * parts * head_dim
    assert up_own.shape[1] == tile
    columns = 3 * tile
    whole = pl.BlockSpec((parts, depth, head_dim), lambda i: (0, 0, 0))
    return pl.pallas_call(
        products_kernel,
        out_shape=tuple(jax.ShapeDtypeStruct((size, columns), dtype) for size, dtype in pieces),
        grid=(3,),
        in_specs=[
            pl.BlockSpec((row_count, depth), lambda i: (0, 0)),
            whole,
            whole,
            pl.BlockSpec((depth, tile), lambda i: (0, 0)),
            pl.BlockSpec((depth, tile), lambda i: (0, 0)),
        ],
        out_specs=tuple(pl.BlockSpec((size, tile), lambda i: (0, i)) for size, _ in pieces),
        scratch_shapes=[pltpu.VMEM((depth, tile), jnp.bfloat16)],
        compiler_params=pltpu.CompilerParams(vmem_limit_bytes=28 << 20),
        cost_estimate=pl.CostEstimate(
            flops=2 * row_count * depth * columns, bytes_accessed=8_000_000, transcendentals=0
        ),
    )(rows, qkv_own, qkv_other, up_own, far_side)


def sum_along_x(two_steps, others, after):
    here, ahead_low, ahead_high, behind_low, behind_high = others
    low, high = lax.optimization_barrier((two_steps, after[:1]))[0]
    first = (shift(low, "x", 1), shift(high, "x", -1))
    ahead_low = (ahead_low + first[0].astype(jnp.float32)).astype(jnp.bfloat16)
    behind_high = (behind_high + first[1].astype(jnp.float32)).astype(jnp.bfloat16)
    ahead = jnp.concatenate([ahead_low, ahead_high], 0)
    behind = jnp.concatenate([behind_low, behind_high], 0)
    ahead, behind = lax.optimization_barrier(((ahead, behind), after[1:]))[0]
    sums = (ahead, behind)
    ahead, behind = shift(ahead, "x", 1), shift(behind, "x", -1)
    return here + ahead.astype(jnp.float32) + behind.astype(jnp.float32), (sums, (ahead, behind))


def share_along_x(value):
    half = value.shape[0] // 2
    behind, ahead = shift(value, "x", 1), shift(value, "x", -1)
    across = [shift(behind[:half], "x", 1), shift(ahead[half:], "x", -1)]
    return jnp.concatenate([value, ahead, behind], 0), jnp.concatenate(across, 0)


def matmul(left, right):
    return jnp.dot(left, right, preferred_element_type=jnp.float32)


def per_device(
    tokens,
    ln_gain,
    oft_skew,
    tenant_of_image,
    w_qkv,
    w_up,
    up_bias,
    q_gain,
    k_gain,
    w_out,
    w_down,
    down_bias,
):
    row_count, local_width = tokens.shape
    head_dim = w_qkv.shape[3]
    qkv_cols = 3 * head_dim
    across, along = lax.axis_size("zh"), lax.axis_size("x")
    group = across * along

    hidden_width = up_bias.shape[0]
    small_own = jnp.concatenate([up_bias[None], q_gain, k_gain], 1)

    floats = tokens.astype(jnp.float32)
    row_sums = jnp.concatenate([jnp.sum(floats, 1), jnp.sum(floats * floats, 1)])[None]
    row_sums = jnp.broadcast_to(row_sums[None], (group, 1, 2 * row_count))
    row_sums = lax.all_to_all(row_sums, GY, 0, 0, tiled=True)

    rotation = cayley(tenant_of_image, oft_skew)
    turned = rotate(tokens, row_sums, ln_gain[None], rotation, local_width * group)

    out_own = w_out.reshape(head_dim, w_out.shape[2])
    qkv_own = w_qkv.transpose(1, 2, 0, 3)[0]
    layers, lines = lax.axis_size("zl"), lax.axis_size("y")
    column = jnp.stack([turned] + [mirror(turned, "zl", mask) for mask in range(1, layers)])
    column, *own = lax.optimization_barrier((column, qkv_own, w_up, w_down, out_own))
    qkv_other, far_side = swap(own[0]), swap(jnp.concatenate(own[1:], 0))
    two_steps, others = reorder(from_ahead(column, "y"), row_source, (4, 12))
    two_steps = two_steps.reshape(-1, local_width)
    others = others.reshape(-1, local_width)
    two_steps, qkv_other, far_side, small_other = lax.optimization_barrier(
        (two_steps, qkv_other, far_side, swap(small_own))
    )
    small = jnp.stack([small_own, small_other])
    bias = small[:, 0, :hidden_width].reshape(2 * hidden_width)
    q_gains = small[:, :, hidden_width : hidden_width + head_dim]
    k_gains = small[:, :, hidden_width + head_dim :]
    second_other = far_side[local_width:]
    second = jnp.concatenate([w_down, second_other[:-head_dim], out_own, second_other[-head_dim:]], 0)
    first = (qkv_own, qkv_other, w_up, far_side)
    sent = (row_count, jnp.bfloat16)
    added = (row_count, jnp.float32)
    half_pieces = ((2 * row_count, jnp.float32), added, sent, sent, added)
    two_steps = products(two_steps, *first, (sent,) * 4)
    others, two_steps = lax.optimization_barrier((others, two_steps))
    others = products(others, *first, half_pieces * 2)
    far_total, came = sum_along_x(two_steps[:2], others[:5], ())
    split = 2 * qkv_cols
    far_total = far_total.astype(jnp.bfloat16)
    far_qkv, far_up = shift(far_total[:, :split], "zh", 1), shift(far_total[:, split:], "zh", 1)
    total, _ = sum_along_x(two_steps[2:], others[5:], came)
    queries, pair = heads(total, far_qkv, q_gains, k_gains)
    attended = attention(queries, pair, swap(pair))
    far_up, pair = lax.optimization_barrier((far_up, pair))
    up_pre = total[:, split:] + far_up.astype(jnp.float32) + bias
    hidden = jax.nn.gelu(up_pre, approximate=False).astype(jnp.bfloat16)

    value = jnp.concatenate([hidden, attended], 1)
    partner = shift(value, "zh", 1)
    given = [jnp.concatenate(share_along_x(value), 0), *share_along_x(partner)]
    parts = [
        matmul(rows, second).astype(jnp.bfloat16).reshape(-1, row_count, local_width) for rows in given
    ]
    outgoing = reorder(parts, owner_source, (layers,) * lines)
    sent = {k: shift(outgoing[k], "y", k) for k in FAR_FIRST}
    total = outgoing[0].astype(jnp.float32)
    for k in FAR_FIRST:
        total = total + sent[k].astype(jnp.float32)
    returned = lax.all_to_all(total.astype(jnp.bfloat16), "zl", 0, 0, tiled=True)
    mixed = jnp.sum(returned.astype(jnp.float32), 0)
    return (floats + mixed + down_bias).astype(jnp.bfloat16)


def solution(mesh):
    names = tuple(name for name, _ in AXES)
    sizes = tuple(size for _, size in AXES)
    fine_mesh = Mesh(mesh.devices.reshape(sizes), names)
    in_specs = (
        P(GX, GY),
        P(GY),
        P(None, GY, None, None),
        P(),
        P(GY, GX, None, None),
        P(GY, GX),
        P(GX),
        P(GX, None),
        P(GX, None),
        P(GX, None, GY),
        P(GX, GY),
        P(GY),
    )
    return jax.shard_map(
        per_device, mesh=fine_mesh, in_specs=in_specs, out_specs=P(GX, GY), check_vma=False
    )
```
